32 devices in a mesh: cuts: 4 (over z), space: 8 (over y, x, core).
Axes of the slice: x: 2, y: 2, z: 4, core: 2. Of those that a mesh axis runs over, the one named last changes fastest.
Arguments:
- states: float32 [4, 256, 2048], P('cuts', 'space'), may hold values from -6 to 6
- stream: float32 [256, 2048], P('space'), may hold values from -4 to 4
Outputs:
- new_states: float32 [4, 256, 2048], P('cuts', 'space')
The draws below stay inside these ranges and needn't reach their ends.
All inputs are finite; a program needn't handle non-finite values.
Results may differ from the reference program's by a relative error of at most 0.00002.
Values sent between devices are 32-bit elements; how exact they have to be, the bound alone decides.
No kernel may reach another device: no remote copies, remote signals or barrier semaphores. Data moves between devices by JAX's collectives and lax.ppermute only.
A program may use at most 64 MiB of HBM per device.

```python
import jax
import jax.numpy as jnp
from jax import lax

COLS = 2048
FINE_STEPS = 4
SLICES = 4
NY = 256


def block_scale(own_key, shape, cuts, low, largest):
    loudness = 1.0
    for axis_at, shards_of in cuts:
        steps = jax.random.uniform(jax.random.fold_in(jax.random.fold_in(own_key, 6), axis_at), (shards_of,), jnp.float32, low / len(cuts), largest / len(cuts))
        loudness = loudness * jnp.repeat(jnp.exp(steps), shape[axis_at] // shards_of).reshape((-1,) + (1,) * (len(shape) - 1 - axis_at))
    return loudness


def bell_draw(key, shape, deviation, reach, split=(), dtype=jnp.bfloat16):
    array = deviation * jax.random.normal(key, shape, jnp.float32)
    if split:
        array = array * block_scale(key, shape, split, -0.22, 0.18)
    return jnp.clip(array, -reach, reach).astype(dtype)


def setup_inputs(seed: int = 0) -> dict:
    seeds = jax.random.split(jax.random.key(seed), 3)
    return {
        "states": bell_draw(seeds[0], (SLICES, NY, COLS), 1.0, 6.0, ((0, 4), (1, 8)), jnp.float32),
        "stream": bell_draw(seeds[1], (NY, COLS), 1.0, 4.0, ((0, 8),), jnp.float32),
    }


VISCOSITY = 0.2
FINE_DT = 0.25


def wrap_rows(field):
    return jnp.concatenate([field[-1:], field, field[:1]], axis=0)


def velocity(padded, spacing):
    middle = padded[1:-1]
    speed_x = (padded[2:] - padded[:-2]) / (2.0 * spacing)
    speed_y = -((jnp.roll(middle, -1, 1) - jnp.roll(middle, 1, 1)) / (2.0 * spacing))
    return speed_x, speed_y


def tendency(padded, speed_x, speed_y, spacing):
    middle = padded[1:-1]
    right_col = jnp.roll(middle, -1, 1)
    left_col = jnp.roll(middle, 1, 1)
    upper_row = padded[2:]
    lower_row = padded[:-2]
    slope_x = (right_col - left_col) / (2.0 * spacing)
    slope_y = (upper_row - lower_row) / (2.0 * spacing)
    laplace = (upper_row + lower_row + right_col + left_col - 4.0 * middle) / (spacing * spacing)
    return -speed_x * slope_x - speed_y * slope_y + VISCOSITY * laplace


def runge_step(field, speed_x, speed_y, spacing, step_size, pad_fn):
    segment_one = tendency(pad_fn(field), speed_x, speed_y, spacing)
    segment_two = tendency(pad_fn(field + (0.5 * step_size) * segment_one), speed_x, speed_y, spacing)
    segment_three = tendency(pad_fn(field + (0.5 * step_size) * segment_two), speed_x, speed_y, spacing)
    segment_four = tendency(pad_fn(field + step_size * segment_three), speed_x, speed_y, spacing)
    return field + (step_size / 6.0) * (segment_one + 2.0 * segment_two + 2.0 * segment_three + segment_four)


def restrict(field):
    leading = field.shape[:-2]
    height, width = field.shape[-2:]
    return field.reshape(leading + (height // 4, 4, width // 4, 4)).mean(axis=(-3, -1))


def prolong(field):
    return jnp.repeat(jnp.repeat(field, 4, axis=-2), 4, axis=-1)


def reference(states, stream):
    fine_u, fine_v = velocity(wrap_rows(stream), 1.0)
    coarse_u, coarse_v = velocity(wrap_rows(restrict(stream)), 4.0)

    def fine_prop(field):
        for _ in range(FINE_STEPS):
            field = runge_step(field, fine_u, fine_v, 1.0, FINE_DT, wrap_rows)
        return field

    def coarse_prop(field):
        return runge_step(field, coarse_u, coarse_v, 4.0, FINE_DT * FINE_STEPS, wrap_rows)

    fine_end = lax.map(fine_prop, states)
    coarse_old = lax.map(lambda field: coarse_prop(restrict(field)), states)
    coarse_gap = restrict(fine_end) - coarse_old
    current = restrict(states[0])
    stepped_all = []
    for member in range(states.shape[0]):
        stepped = coarse_prop(current)
        stepped_all.append(stepped)
        current = stepped + coarse_gap[member]
    return fine_end + prolong(jnp.stack(stepped_all) - coarse_old)
```

```python
import functools

import jax
import jax.numpy as jnp
from jax import lax
from jax.experimental import pallas as pl
from jax.experimental.pallas import tpu as pltpu
from jax.sharding import PartitionSpec as P

FINE_STEPS = 4
VISCOSITY = 0.2
FINE_DT = 0.25
BLOCK = 4
LANES = 128
SUB = 8
STAGES = 4
REACH = FINE_STEPS * STAGES // 2
SPILL = REACH // BLOCK
VMEM = pl.BlockSpec(memory_space=pltpu.VMEM)
UNROLL = 16


def lane_index(shape):
    return lax.broadcasted_iota(jnp.int32, shape, len(shape) - 1)


def set_coefs(psi, coefs, rows, scale, diffusion):
    tiles = psi.shape[0]
    lo, hi = rows
    lane = lane_index((hi - lo, LANES))

    def body(t, _):
        after, before = lax.rem(t + 1, tiles), lax.rem(t + tiles - 1, tiles)
        here = psi[t, lo:hi]
        east = jnp.where(lane == LANES - 1, pltpu.roll(psi[after, lo:hi], LANES - 1, 1), pltpu.roll(here, LANES - 1, 1))
        west = jnp.where(lane == 0, pltpu.roll(psi[before, lo:hi], 1, 1), pltpu.roll(here, 1, 1))
        u = scale * (psi[t, lo + 1 : hi + 1] - psi[t, lo - 1 : hi - 1])
        v = -scale * (east - west)
        coefs[0, t, lo:hi] = diffusion - u
        coefs[1, t, lo:hi] = diffusion + u
        coefs[2, t, lo:hi] = diffusion - v
        coefs[3, t, lo:hi] = diffusion + v
        return 0

    lax.fori_loop(0, tiles, body, 0, unroll=min(tiles, UNROLL))


def stage(source, coefs, rows, diffusion, finish):
    tiles = source.shape[0]
    lo, hi = rows
    lane = lane_index((hi - lo, LANES))
    first, last = lane == 0, lane == LANES - 1

    def body(t, carry):
        here, to_east, from_west = carry
        after = source[lax.rem(t + 1, tiles), lo:hi]
        after_east = pltpu.roll(after, LANES - 1, 1)
        to_west = pltpu.roll(here, 1, 1)
        east = jnp.where(last, after_east, to_east)
        west = jnp.where(first, from_west, to_west)
        out = (coefs[0, t, lo:hi] * east + coefs[1, t, lo:hi] * west) + (
            coefs[2, t, lo:hi] * source[t, lo + 1 : hi + 1] + coefs[3, t, lo:hi] * source[t, lo - 1 : hi - 1]
        )
        finish(t, out, here)
        return after, after_east, to_west

    here = source[0, lo:hi]
    carry = (here, pltpu.roll(here, LANES - 1, 1), pltpu.roll(source[tiles - 1, lo:hi], 1, 1))
    lax.fori_loop(0, tiles, body, carry, unroll=min(tiles, UNROLL))


def step(a, z, coefs, rows, diffusion, last_rows=None):
    centre = 4.0 * diffusion
    lo, hi = rows

    def one(t, out, here):
        z[0, t, lo:hi] = out + (4.0 - centre) * here

    def two(t, out, here):
        z[1, t, lo:hi] = (out - centre * here) + 12.0 * a[t, lo:hi]

    def three(t, out, here):
        z[0, t, lo:hi] = (out - centre * here) + 24.0 * a[t, lo:hi]

    low, high = last_rows or rows

    def four(t, out, here):
        a[t, low:high] = a[t, low:high] + (out - centre * here) * (1.0 / 24.0)

    stage(a, coefs, rows, diffusion, one)
    stage(z.at[0], coefs, rows, diffusion, two)
    stage(z.at[1], coefs, rows, diffusion, three)
    stage(z.at[0], coefs, (low, high), diffusion, four)


def pooled(take, rows, tiles, put):
    lane = lane_index((rows, LANES))
    pick = lax.rem(lane * BLOCK, LANES)
    per = LANES // BLOCK

    def body(k, _):
        out = jnp.zeros((rows, LANES), jnp.float32)
        for q in range(BLOCK):
            t = k * BLOCK + q
            s = (take(t, 0) + take(t, 1)) + (take(t, 2) + take(t, 3))
            s = s + pltpu.roll(s, LANES - 1, 1)
            s = s + pltpu.roll(s, LANES - 2, 1)
            s = jnp.take_along_axis(s, pick, axis=1)
            out = jnp.where((lane >= q * per) & (lane < (q + 1) * per), s, out)
        put(k, out * (1.0 / (BLOCK * BLOCK)))
        return 0

    lax.fori_loop(0, tiles // BLOCK, body, 0)


def pre_kernel(states, stream, out, tall):
    rows, cols = states.shape
    count = rows // BLOCK
    for k, source in enumerate((states, stream)):
        for t in range(cols // LANES):
            tall[k, t] = source[:, t * LANES : (t + 1) * LANES]

        def take(t, i, k=k):
            return tall[k, t, pl.ds(i, count, stride=BLOCK)]

        def put(t, value, k=k):
            out[t, k * count : (k + 1) * count] = value

        pooled(take, count, cols // LANES, put)


def pre_call(states, stream):
    rows, cols = states.shape
    tiles = cols // LANES
    return pl.pallas_call(
        pre_kernel,
        out_shape=jax.ShapeDtypeStruct((tiles // BLOCK, 2 * rows // BLOCK, LANES), jnp.float32),
        in_specs=[VMEM] * 2,
        out_specs=VMEM,
        scratch_shapes=[pltpu.VMEM((2, tiles, rows, LANES), jnp.float32)],
        name="restrict",
    )(states, stream)


def fine_kernel(states, stream, low, high, fine, edge_low, edge_high, e_out, a, psi, z, coefs):
    rows, cols = states.shape
    tiles = cols // LANES
    own = SUB + REACH
    top = own + rows
    size = a.shape[1]
    for t in range(tiles):
        at = slice(t * LANES, (t + 1) * LANES)
        for buffer, source, k in ((a, states, 0), (psi, stream, 1)):
            buffer[t, 0:SUB] = jnp.zeros((SUB, LANES), jnp.float32)
            buffer[t, SUB:own] = low[k * REACH : (k + 1) * REACH, at]
            buffer[t, own:top] = source[:, at]
            buffer[t, top : top + REACH] = high[k * REACH : (k + 1) * REACH, at]
            buffer[t, top + REACH : size] = jnp.zeros((size - top - REACH, LANES), jnp.float32)
        for k in range(2):
            z[k, t, 0:SUB] = jnp.zeros((SUB, LANES), jnp.float32)
            z[k, t, top + REACH : size] = jnp.zeros((size - top - REACH, LANES), jnp.float32)
    span = (SUB, top + REACH)
    diffusion = VISCOSITY * FINE_DT
    set_coefs(psi, coefs, span, FINE_DT * 0.25, diffusion)
    half = FINE_STEPS // 2
    for n in range(half):
        step(a, z, coefs, span, diffusion, (own, top) if n == half - 1 else None)
    for t in range(tiles):
        a[t, SUB:own] = jnp.zeros((REACH, LANES), jnp.float32)
        a[t, top : top + REACH] = jnp.zeros((REACH, LANES), jnp.float32)
    for n in range(FINE_STEPS - half):
        step(a, z, coefs, span, diffusion)
    for t in range(tiles):
        fine[t] = a[t, own:top]
        edge_low[t] = a[t, SUB:own]
        edge_high[t] = a[t, top : top + REACH]
    spread = e_out.shape[1]

    def take(t, i):
        return a[t, pl.ds(SUB + i, spread, stride=BLOCK)]

    def put(k, value):
        e_out[k] = value

    pooled(take, spread, tiles, put)


def fine_call(states, stream, low, high):
    rows, cols = states.shape
    tiles = cols // LANES
    spread = -(-(rows // BLOCK + 2 * SPILL) // SUB) * SUB
    size = SUB + max(BLOCK * spread, rows + 2 * REACH + SUB)
    f32 = jnp.float32
    return pl.pallas_call(
        fine_kernel,
        out_shape=(
            jax.ShapeDtypeStruct((tiles, rows, LANES), f32),
            jax.ShapeDtypeStruct((tiles, REACH, LANES), f32),
            jax.ShapeDtypeStruct((tiles, REACH, LANES), f32),
            jax.ShapeDtypeStruct((tiles // BLOCK, spread, LANES), f32),
        ),
        in_specs=[VMEM] * 4,
        out_specs=(VMEM,) * 4,
        scratch_shapes=[
            pltpu.VMEM((tiles, size, LANES), f32),
            pltpu.VMEM((tiles, size, LANES), f32),
            pltpu.VMEM((2, tiles, size, LANES), f32),
            pltpu.VMEM((4, tiles, size, LANES), f32),
        ],
        name="fine",
    )(states, stream, low, high)


def pair_kernel(mine, theirs, out):
    tiles, both, _ = mine.shape
    rows = both // 2
    odd = lax.rem(lax.axis_index("space"), 2) == 1
    for t in range(tiles):
        lower = jnp.where(odd, theirs[t], mine[t])
        upper = jnp.where(odd, mine[t], theirs[t])
        for k in range(2):
            out[t, 2 * k * rows : (2 * k + 1) * rows] = lower[k * rows : (k + 1) * rows]
            out[t, (2 * k + 1) * rows : (2 * k + 2) * rows] = upper[k * rows : (k + 1) * rows]


def pair_call(mine, theirs):
    tiles, both, _ = mine.shape
    return pl.pallas_call(
        pair_kernel,
        out_shape=jax.ShapeDtypeStruct((tiles, 2 * both, LANES), jnp.float32),
        in_specs=[VMEM] * 2,
        out_specs=VMEM,
        name="pair",
    )(mine, theirs)


def spread_kernel(rows, mine, theirs, whole, message):
    tiles, spread, _ = mine.shape
    odd = lax.rem(lax.axis_index("space"), 2) == 1
    for t in range(tiles):
        lower = jnp.where(odd, theirs[t], mine[t])
        upper = jnp.where(odd, mine[t], theirs[t])
        whole[t, 0:spread] = lower
        whole[t, spread:] = jnp.zeros((whole.shape[1] - spread, LANES), jnp.float32)
        whole[t, rows : rows + spread] = whole[t, rows : rows + spread] + upper
        message[t] = jnp.where(odd, whole[t, 2 * SPILL : 2 * SPILL + 2 * rows], whole[t, 0 : 2 * rows])


def spread_call(mine, theirs, rows):
    tiles, spread, _ = mine.shape
    f32 = jnp.float32
    return pl.pallas_call(
        functools.partial(spread_kernel, rows),
        out_shape=(
            jax.ShapeDtypeStruct((tiles, rows + spread, LANES), f32),
            jax.ShapeDtypeStruct((tiles, 2 * rows, LANES), f32),
        ),
        in_specs=[VMEM] * 2,
        out_specs=(VMEM,) * 2,
        name="spread",
    )(mine, theirs)


def partner(n, k, size):
    return n ^ k if size & (size - 1) == 0 else (n + k) % size


def chain(pads, outs, rows, scratch):
    gap, old, psi, z, coefs, powers = scratch
    tiles, size, _ = gap.shape
    spacing, length = float(BLOCK), FINE_DT * FINE_STEPS
    diffusion = VISCOSITY * length / (spacing * spacing)
    whole = (SUB, size - SUB)
    base = SUB + pads
    slices = len(outs)
    own = base + pl.multiple_of(rows * lax.rem(lax.axis_index("space"), 2), SUB)
    set_coefs(psi, coefs, whole, length / (2.0 * spacing) / (2.0 * spacing), diffusion)
    step(old, z, coefs, whole, diffusion)
    n = lax.axis_index("cuts")
    for t in range(tiles):
        start = jnp.where(n == 0, old[t, whole[0] : whole[1]], 0.0)
        gap[t, whole[0] : whole[1]] = (gap[t, whole[0] : whole[1]] - old[t, whole[0] : whole[1]]) + start
        mine = old[t, pl.ds(own, rows)]
        outs[-1][t] = jnp.where(n == 0, mine, 0.0) - mine
    reach = STAGES * (slices - 1)

    def around(extent):
        extent = min(-(-extent // SUB) * SUB, pads)
        return (base - extent, base + 2 * rows + extent)

    for j in range(1, slices):
        reach -= STAGES
        step(gap, z, coefs, around(reach + STAGES - 1), diffusion, around(reach))
        for t in range(tiles):
            powers[j, t] = gap[t, pl.ds(own, rows)]
    for k in range(1, slices):
        ahead = jnp.clip(partner(n, k, slices) - n, 1, slices - 1)
        for t in range(tiles):
            outs[k - 1][t] = powers[ahead, t]


def pair_chain_kernel(slices, rows, whole, message, passed, coarse, coarse_near, coarse_far, *refs):
    outs, scratch = refs[:slices], refs[slices:]
    gap, old, psi, z = scratch[:4]
    tiles = gap.shape[0]
    size = gap.shape[1]
    odd = lax.rem(lax.axis_index("space"), 2) == 1
    pads = 2 * rows
    base = SUB + pads
    edge = jnp.zeros((SUB, LANES), jnp.float32)
    for t in range(tiles):
        before, after = jnp.where(odd, passed[t], message[t]), jnp.where(odd, message[t], passed[t])
        gap[t] = jnp.zeros((size, LANES), jnp.float32)
        at = base - SPILL
        gap[t, at : at + whole.shape[1]] = whole[t]
        at = base + SPILL - 2 * rows
        gap[t, at : at + 2 * rows] = gap[t, at : at + 2 * rows] + before
        at = base - SPILL + 2 * rows
        gap[t, at : at + 2 * rows] = gap[t, at : at + 2 * rows] + after
        before = jnp.where(odd, coarse_far[t], coarse_near[t])
        after = jnp.where(odd, coarse_near[t], coarse_far[t])
        for k, out in ((0, old), (1, psi)):
            part = slice(2 * k * rows, 2 * (k + 1) * rows)
            out[t, 0:SUB] = edge
            out[t, SUB:base] = before[part]
            out[t, base : base + 2 * rows] = coarse[t, part]
            out[t, base + 2 * rows : base + 4 * rows] = after[part]
            out[t, size - SUB : size] = edge
        for k in range(2):
            z[k, t, 0:SUB] = edge
            z[k, t, size - SUB : size] = edge
    chain(pads, outs, rows, scratch)


def chain_scratch(tiles, size, slices, rows):
    f32 = jnp.float32
    return [
        pltpu.VMEM((tiles, size, LANES), f32),
        pltpu.VMEM((tiles, size, LANES), f32),
        pltpu.VMEM((tiles, size, LANES), f32),
        pltpu.VMEM((2, tiles, size, LANES), f32),
        pltpu.VMEM((4, tiles, size, LANES), f32),
        pltpu.VMEM((slices, tiles, rows, LANES), f32),
    ]


def pair_chain_call(slices, whole, message, passed, coarse, coarse_near, coarse_far):
    tiles = whole.shape[0]
    rows = message.shape[1] // 2
    return pl.pallas_call(
        functools.partial(pair_chain_kernel, slices, rows),
        out_shape=(jax.ShapeDtypeStruct((tiles, rows, LANES), jnp.float32),) * slices,
        in_specs=[VMEM] * 6,
        out_specs=(VMEM,) * slices,
        scratch_shapes=chain_scratch(tiles, 6 * rows + 2 * SUB, slices, rows),
        name="coarse",
    )(whole, message, passed, coarse, coarse_near, coarse_far)


def wide_chain_kernel(slices, rows, gap_in, old_in, psi_in, *refs):
    outs, scratch = refs[:slices], refs[slices:]
    gap, old, psi, z = scratch[:4]
    tiles, size, _ = gap.shape
    edge = jnp.zeros((SUB, LANES), jnp.float32)
    for t in range(tiles):
        for source, out in ((gap_in, gap), (old_in, old), (psi_in, psi)):
            out[t, 0:SUB] = edge
            out[t, SUB : size - SUB] = source[t]
            out[t, size - SUB : size] = edge
        for k in range(2):
            z[k, t, 0:SUB] = edge
            z[k, t, size - SUB : size] = edge
    chain((size - 2 * SUB - 2 * rows) // 2, outs, rows, scratch)


def wide_chain(slices, spread, coarse):
    tiles, both, _ = coarse.shape
    rows = both // 2
    bands = lax.axis_size("space")
    total = bands * rows
    length = spread.shape[1]
    every = lax.all_gather(spread, "space")
    gap = jnp.zeros((tiles, total, LANES), jnp.float32)
    for b in range(bands):
        at = (b * rows - SPILL + jnp.arange(length)) % total
        gap = gap.at[:, at].add(every[b])
    every = lax.all_gather(coarse, "space")
    old, psi = (jnp.moveaxis(every[:, :, k * rows : (k + 1) * rows], 0, 1).reshape(tiles, total, LANES) for k in range(2))
    pads = STAGES * slices
    first = lax.axis_index("space") // 2 * 2 * rows
    at = (first - pads + jnp.arange(2 * rows + 2 * pads)) % total
    size = 2 * rows + 2 * pads + 2 * SUB
    return pl.pallas_call(
        functools.partial(wide_chain_kernel, slices, rows),
        out_shape=(jax.ShapeDtypeStruct((tiles, rows, LANES), jnp.float32),) * slices,
        in_specs=[VMEM] * 3,
        out_specs=(VMEM,) * slices,
        scratch_shapes=chain_scratch(tiles, size, slices, rows),
        name="coarse",
    )(*(jnp.take(x, at, axis=1) for x in (gap, old, psi)))


def out_kernel(slices, fine, from_low, from_high, own, *refs):
    received, (out, tall) = refs[: slices - 1], refs[slices - 1 :]
    tiles, rows, _ = fine.shape
    count = rows // BLOCK
    n = lax.axis_index("cuts")
    lane = lane_index((count, LANES))
    per = LANES // BLOCK
    sources = [(n ^ k) if slices & (slices - 1) == 0 else lax.rem(n + slices - k, slices) for k in range(1, slices)]
    for k in range(tiles // BLOCK):
        total = own[k]
        for source, x in zip(sources, received, strict=True):
            total = total + jnp.where(source < n, x[k], 0.0)
        for q in range(BLOCK):
            t = k * BLOCK + q
            up = jnp.take_along_axis(total, q * per + lane // BLOCK, axis=1)
            for i in range(BLOCK):
                tall[t, pl.ds(i, count, stride=BLOCK)] = up
    for t in range(tiles):
        at = slice(t * LANES, (t + 1) * LANES)
        out[0, 0:REACH, at] = (fine[t, 0:REACH] + from_low[t]) + tall[t, 0:REACH]
        out[0, REACH : rows - REACH, at] = fine[t, REACH : rows - REACH] + tall[t, REACH : rows - REACH]
        out[0, rows - REACH : rows, at] = (fine[t, rows - REACH : rows] + from_high[t]) + tall[t, rows - REACH : rows]


def out_call(slices, fine, from_low, from_high, own, received):
    tiles, rows, _ = fine.shape
    return pl.pallas_call(
        functools.partial(out_kernel, slices),
        out_shape=jax.ShapeDtypeStruct((1, rows, tiles * LANES), jnp.float32),
        in_specs=[VMEM] * (3 + slices),
        out_specs=VMEM,
        scratch_shapes=[pltpu.VMEM((tiles, rows, LANES), jnp.float32)],
        name="total",
    )(fine, from_low, from_high, own, *received)


def per_device(states, stream):
    state = states[0]
    slices, bands = lax.axis_size("cuts"), lax.axis_size("space")
    rows = state.shape[0] // BLOCK
    up = [(i, (i + 1) % bands) for i in range(bands)]
    down = [(i, (i - 1) % bands) for i in range(bands)]
    twin = [(i, i ^ 1) for i in range(bands)]
    across = [(i, (i + 1 if i % 2 else i - 1) % bands) for i in range(bands)]

    def exchange(x, pairs):
        return lax.ppermute(x, "space", pairs)

    low = exchange(jnp.concatenate([state[-REACH:], stream[-REACH:]]), up)
    high = exchange(jnp.concatenate([state[:REACH], stream[:REACH]]), down)
    coarse = pre_call(state, stream)
    paired = bands % 2 == 0 and STAGES * (slices - 1) <= 2 * rows - SPILL
    if paired:
        coarse = pair_call(coarse, exchange(coarse, twin))
        coarse_near = exchange(coarse, across)
        coarse_far = exchange(coarse_near, twin)
    fine, edge_low, edge_high, spread = fine_call(state, stream, low, high)
    if paired:
        whole, message = spread_call(spread, exchange(spread, twin), rows)
        near = exchange(message, across)
        far = exchange(near, twin)
        from_low, from_high = exchange(edge_high, up), exchange(edge_low, down)
        *sent, own = pair_chain_call(slices, whole, near, far, coarse, coarse_near, coarse_far)
    else:
        from_low, from_high = exchange(edge_high, up), exchange(edge_low, down)
        *sent, own = wide_chain(slices, spread, coarse)
    received = [
        lax.ppermute(x, "cuts", [(i, partner(i, k, slices)) for i in range(slices)]) for k, x in enumerate(sent, 1)
    ]
    return out_call(slices, fine, from_low, from_high, own, received)


def solution(mesh):
    return jax.shard_map(
        per_device,
        mesh=mesh,
        in_specs=(P("cuts", "space", None), P("space", None)),
        out_specs=P("cuts", "space", None),
        check_vma=False,
    )
```

```python
import functools

import jax
import jax.numpy as jnp
from jax import lax
from jax.experimental import pallas as pl
from jax.experimental.pallas import tpu as pltpu
from jax.sharding import PartitionSpec as P

FINE_STEPS = 4
VISCOSITY = 0.2
FINE_DT = 0.25
BLOCK = 4
LANES = 128
SUB = 8
STAGES = 4
REACH = FINE_STEPS * STAGES // 2
SPILL = REACH // BLOCK
VMEM = pl.BlockSpec(memory_space=pltpu.VMEM)
UNROLL = 16
COMPACT = pltpu.CompilerParams(vmem_limit_bytes=12 * 2**20)


def lane_index(shape):
    return lax.broadcasted_iota(jnp.int32, shape, len(shape) - 1)


def set_coefs(psi, coefs, rows, scale, diffusion):
    tiles = psi.shape[0]
    lo, hi = rows
    lane = lane_index((hi - lo, LANES))

    def body(t, _):
        after, before = lax.rem(t + 1, tiles), lax.rem(t + tiles - 1, tiles)
        here = psi[t, lo:hi]
        east = jnp.where(lane == LANES - 1, pltpu.roll(psi[after, lo:hi], LANES - 1, 1), pltpu.roll(here, LANES - 1, 1))
        west = jnp.where(lane == 0, pltpu.roll(psi[before, lo:hi], 1, 1), pltpu.roll(here, 1, 1))
        u = scale * (psi[t, lo + 1 : hi + 1] - psi[t, lo - 1 : hi - 1])
        v = -scale * (east - west)
        coefs[0, t, lo:hi] = diffusion - u
        coefs[1, t, lo:hi] = diffusion + u
        coefs[2, t, lo:hi] = diffusion - v
        coefs[3, t, lo:hi] = diffusion + v
        return 0

    lax.fori_loop(0, tiles, body, 0, unroll=min(tiles, UNROLL))


def stage(source, coefs, rows, diffusion, finish):
    tiles = source.shape[0]
    lo, hi = rows
    lane = lane_index((hi - lo, LANES))
    first, last = lane == 0, lane == LANES - 1

    def body(t, carry):
        here, to_east, from_west = carry
        after = source[lax.rem(t + 1, tiles), lo:hi]
        after_east = pltpu.roll(after, LANES - 1, 1)
        to_west = pltpu.roll(here, 1, 1)
        east = jnp.where(last, after_east, to_east)
        west = jnp.where(first, from_west, to_west)
        out = (coefs[0, t, lo:hi] * east + coefs[1, t, lo:hi] * west) + (
            coefs[2, t, lo:hi] * source[t, lo + 1 : hi + 1] + coefs[3, t, lo:hi] * source[t, lo - 1 : hi - 1]
        )
        finish(t, out, here)
        return after, after_east, to_west

    here = source[0, lo:hi]
    carry = (here, pltpu.roll(here, LANES - 1, 1), pltpu.roll(source[tiles - 1, lo:hi], 1, 1))
    lax.fori_loop(0, tiles, body, carry, unroll=min(tiles, UNROLL))


def step(a, z, coefs, rows, diffusion, last_rows=None):
    centre = 4.0 * diffusion
    lo, hi = rows

    def one(t, out, here):
        z[0, t, lo:hi] = out + (4.0 - centre) * here

    def two(t, out, here):
        z[1, t, lo:hi] = (out - centre * here) + 12.0 * a[t, lo:hi]

    def three(t, out, here):
        z[0, t, lo:hi] = (out - centre * here) + 24.0 * a[t, lo:hi]

    low, high = last_rows or rows

    def four(t, out, here):
        a[t, low:high] = a[t, low:high] + (out - centre * here) * (1.0 / 24.0)

    stage(a, coefs, rows, diffusion, one)
    stage(z.at[0], coefs, rows, diffusion, two)
    stage(z.at[1], coefs, rows, diffusion, three)
    stage(z.at[0], coefs, (low, high), diffusion, four)


def pooled(take, rows, tiles, put):
    lane = lane_index((rows, LANES))
    pick = lax.rem(lane * BLOCK, LANES)
    per = LANES // BLOCK

    for k in range(tiles // BLOCK):
        out = jnp.zeros((rows, LANES), jnp.float32)
        for q in range(BLOCK):
            t = k * BLOCK + q
            s = (take(t, 0) + take(t, 1)) + (take(t, 2) + take(t, 3))
            s = s + pltpu.roll(s, LANES - 1, 1)
            s = s + pltpu.roll(s, LANES - 2, 1)
            s = jnp.take_along_axis(s, pick, axis=1)
            out = jnp.where((lane >= q * per) & (lane < (q + 1) * per), s, out)
        put(k, out * (1.0 / (BLOCK * BLOCK)))


def pre_kernel(states, stream, out, tall):
    rows, cols = states.shape
    count = rows // BLOCK
    for k, source in enumerate((states, stream)):
        for t in range(cols // LANES):
            tall[k, t] = source[:, t * LANES : (t + 1) * LANES]

        def take(t, i, k=k):
            return tall[k, t, pl.ds(i, count, stride=BLOCK)]

        def put(t, value, k=k):
            out[t, k * count : (k + 1) * count] = value

        pooled(take, count, cols // LANES, put)


def pre_call(states, stream):
    rows, cols = states.shape
    tiles = cols // LANES
    return pl.pallas_call(
        pre_kernel,
        out_shape=jax.ShapeDtypeStruct((tiles // BLOCK, 2 * rows // BLOCK, LANES), jnp.float32),
        in_specs=[VMEM] * 2,
        out_specs=VMEM,
        scratch_shapes=[pltpu.VMEM((2, tiles, rows, LANES), jnp.float32)],
        compiler_params=COMPACT,
        name="restrict",
    )(states, stream)


def fine_kernel(states, stream, low, high, fine, edge_low, edge_high, e_out, a, psi, z, coefs):
    rows, cols = states.shape
    tiles = cols // LANES
    own = SUB + REACH
    top = own + rows
    size = a.shape[1]
    for t in range(tiles):
        at = slice(t * LANES, (t + 1) * LANES)
        for buffer, source, k in ((a, states, 0), (psi, stream, 1)):
            buffer[t, 0:SUB] = jnp.zeros((SUB, LANES), jnp.float32)
            buffer[t, SUB:own] = low[k * REACH : (k + 1) * REACH, at]
            buffer[t, own:top] = source[:, at]
            buffer[t, top : top + REACH] = high[k * REACH : (k + 1) * REACH, at]
            buffer[t, top + REACH : size] = jnp.zeros((size - top - REACH, LANES), jnp.float32)
        for k in range(2):
            z[k, t, 0:SUB] = jnp.zeros((SUB, LANES), jnp.float32)
            z[k, t, top + REACH : size] = jnp.zeros((size - top - REACH, LANES), jnp.float32)
    span = (SUB, top + REACH)
    diffusion = VISCOSITY * FINE_DT
    set_coefs(psi, coefs, span, FINE_DT * 0.25, diffusion)
    half = FINE_STEPS // 2
    for n in range(half):
        step(a, z, coefs, span, diffusion, (own, top) if n == half - 1 else None)
    for t in range(tiles):
        a[t, SUB:own] = jnp.zeros((REACH, LANES), jnp.float32)
        a[t, top : top + REACH] = jnp.zeros((REACH, LANES), jnp.float32)
    for n in range(FINE_STEPS - half):
        step(a, z, coefs, span, diffusion)
    for t in range(tiles):
        fine[t] = a[t, own:top]
        edge_low[t] = a[t, SUB:own]
        edge_high[t] = a[t, top : top + REACH]
    spread = e_out.shape[1]

    def take(t, i):
        return a[t, pl.ds(SUB + i, spread, stride=BLOCK)]

    def put(k, value):
        e_out[k] = value

    pooled(take, spread, tiles, put)


def fine_call(states, stream, low, high):
    rows, cols = states.shape
    tiles = cols // LANES
    spread = -(-(rows // BLOCK + 2 * SPILL) // SUB) * SUB
    size = SUB + max(BLOCK * spread, rows + 2 * REACH + SUB)
    f32 = jnp.float32
    return pl.pallas_call(
        fine_kernel,
        out_shape=(
            jax.ShapeDtypeStruct((tiles, rows, LANES), f32),
            jax.ShapeDtypeStruct((tiles, REACH, LANES), f32),
            jax.ShapeDtypeStruct((tiles, REACH, LANES), f32),
            jax.ShapeDtypeStruct((tiles // BLOCK, spread, LANES), f32),
        ),
        in_specs=[VMEM] * 4,
        out_specs=(VMEM,) * 4,
        scratch_shapes=[
            pltpu.VMEM((tiles, size, LANES), f32),
            pltpu.VMEM((tiles, size, LANES), f32),
            pltpu.VMEM((2, tiles, size, LANES), f32),
            pltpu.VMEM((4, tiles, size, LANES), f32),
        ],
        compiler_params=COMPACT,
        name="fine",
    )(states, stream, low, high)


def pair_kernel(mine, theirs, out):
    tiles, both, _ = mine.shape
    rows = both // 2
    odd = lax.rem(lax.axis_index("space"), 2) == 1
    for t in range(tiles):
        lower = jnp.where(odd, theirs[t], mine[t])
        upper = jnp.where(odd, mine[t], theirs[t])
        for k in range(2):
            out[t, 2 * k * rows : (2 * k + 1) * rows] = lower[k * rows : (k + 1) * rows]
            out[t, (2 * k + 1) * rows : (2 * k + 2) * rows] = upper[k * rows : (k + 1) * rows]


def pair_call(mine, theirs):
    tiles, both, _ = mine.shape
    return pl.pallas_call(
        pair_kernel,
        out_shape=jax.ShapeDtypeStruct((tiles, 2 * both, LANES), jnp.float32),
        in_specs=[VMEM] * 2,
        out_specs=VMEM,
        compiler_params=COMPACT,
        name="pair",
    )(mine, theirs)


def spread_kernel(rows, mine, theirs, whole, message):
    tiles, spread, _ = mine.shape
    odd = lax.rem(lax.axis_index("space"), 2) == 1
    for t in range(tiles):
        lower = jnp.where(odd, theirs[t], mine[t])
        upper = jnp.where(odd, mine[t], theirs[t])
        whole[t, 0:spread] = lower
        whole[t, spread:] = jnp.zeros((whole.shape[1] - spread, LANES), jnp.float32)
        whole[t, rows : rows + spread] = whole[t, rows : rows + spread] + upper
        message[t] = jnp.where(odd, whole[t, 2 * SPILL : 2 * SPILL + 2 * rows], whole[t, 0 : 2 * rows])


def spread_call(mine, theirs, rows):
    tiles, spread, _ = mine.shape
    f32 = jnp.float32
    return pl.pallas_call(
        functools.partial(spread_kernel, rows),
        out_shape=(
            jax.ShapeDtypeStruct((tiles, rows + spread, LANES), f32),
            jax.ShapeDtypeStruct((tiles, 2 * rows, LANES), f32),
        ),
        in_specs=[VMEM] * 2,
        out_specs=(VMEM,) * 2,
        compiler_params=COMPACT,
        name="spread",
    )(mine, theirs)


def partner(n, k, size):
    return n ^ k if size & (size - 1) == 0 else (n + k) % size


def chain(pads, outs, rows, scratch):
    gap, old, psi, z, coefs, powers = scratch
    tiles, size, _ = gap.shape
    spacing, length = float(BLOCK), FINE_DT * FINE_STEPS
    diffusion = VISCOSITY * length / (spacing * spacing)
    whole = (SUB, size - SUB)
    base = SUB + pads
    slices = len(outs)
    own = base + pl.multiple_of(rows * lax.rem(lax.axis_index("space"), 2), SUB)
    set_coefs(psi, coefs, whole, length / (2.0 * spacing) / (2.0 * spacing), diffusion)
    step(old, z, coefs, whole, diffusion)
    n = lax.axis_index("cuts")
    for t in range(tiles):
        start = jnp.where(n == 0, old[t, whole[0] : whole[1]], 0.0)
        gap[t, whole[0] : whole[1]] = (gap[t, whole[0] : whole[1]] - old[t, whole[0] : whole[1]]) + start
        mine = old[t, pl.ds(own, rows)]
        outs[-1][t] = jnp.where(n == 0, mine, 0.0) - mine
    reach = STAGES * (slices - 1)

    def around(extent):
        extent = min(-(-extent // SUB) * SUB, pads)
        return (base - extent, base + 2 * rows + extent)

    for j in range(1, slices):
        reach -= STAGES
        step(gap, z, coefs, around(reach + STAGES - 1), diffusion, around(reach))
        for t in range(tiles):
            powers[j, t] = gap[t, pl.ds(own, rows)]
    for k in range(1, slices):
        ahead = jnp.clip(partner(n, k, slices) - n, 1, slices - 1)
        for t in range(tiles):
            outs[k - 1][t] = powers[ahead, t]


def pair_chain_kernel(slices, rows, whole, message, passed, coarse, coarse_near, coarse_far, *refs):
    outs, scratch = refs[:slices], refs[slices:]
    gap, old, psi, z = scratch[:4]
    tiles = gap.shape[0]
    size = gap.shape[1]
    odd = lax.rem(lax.axis_index("space"), 2) == 1
    pads = 2 * rows
    base = SUB + pads
    edge = jnp.zeros((SUB, LANES), jnp.float32)
    for t in range(tiles):
        before, after = jnp.where(odd, passed[t], message[t]), jnp.where(odd, message[t], passed[t])
        gap[t] = jnp.zeros((size, LANES), jnp.float32)
        at = base - SPILL
        gap[t, at : at + whole.shape[1]] = whole[t]
        at = base + SPILL - 2 * rows
        gap[t, at : at + 2 * rows] = gap[t, at : at + 2 * rows] + before
        at = base - SPILL + 2 * rows
        gap[t, at : at + 2 * rows] = gap[t, at : at + 2 * rows] + after
        before = jnp.where(odd, coarse_far[t], coarse_near[t])
        after = jnp.where(odd, coarse_near[t], coarse_far[t])
        for k, out in ((0, old), (1, psi)):
            part = slice(2 * k * rows, 2 * (k + 1) * rows)
            out[t, 0:SUB] = edge
            out[t, SUB:base] = before[part]
            out[t, base : base + 2 * rows] = coarse[t, part]
            out[t, base + 2 * rows : base + 4 * rows] = after[part]
            out[t, size - SUB : size] = edge
        for k in range(2):
            z[k, t, 0:SUB] = edge
            z[k, t, size - SUB : size] = edge
    chain(pads, outs, rows, scratch)


def chain_scratch(tiles, size, slices, rows):
    f32 = jnp.float32
    return [
        pltpu.VMEM((tiles, size, LANES), f32),
        pltpu.VMEM((tiles, size, LANES), f32),
        pltpu.VMEM((tiles, size, LANES), f32),
        pltpu.VMEM((2, tiles, size, LANES), f32),
        pltpu.VMEM((4, tiles, size, LANES), f32),
        pltpu.VMEM((slices, tiles, rows, LANES), f32),
    ]


def pair_chain_call(slices, whole, message, passed, coarse, coarse_near, coarse_far):
    tiles = whole.shape[0]
    rows = message.shape[1] // 2
    return pl.pallas_call(
        functools.partial(pair_chain_kernel, slices, rows),
        out_shape=(jax.ShapeDtypeStruct((tiles, rows, LANES), jnp.float32),) * slices,
        in_specs=[VMEM] * 6,
        out_specs=(VMEM,) * slices,
        scratch_shapes=chain_scratch(tiles, 6 * rows + 2 * SUB, slices, rows),
        compiler_params=COMPACT,
        name="coarse",
    )(whole, message, passed, coarse, coarse_near, coarse_far)


def wide_chain_kernel(slices, rows, gap_in, old_in, psi_in, *refs):
    outs, scratch = refs[:slices], refs[slices:]
    gap, old, psi, z = scratch[:4]
    tiles, size, _ = gap.shape
    edge = jnp.zeros((SUB, LANES), jnp.float32)
    for t in range(tiles):
        for source, out in ((gap_in, gap), (old_in, old), (psi_in, psi)):
            out[t, 0:SUB] = edge
            out[t, SUB : size - SUB] = source[t]
            out[t, size - SUB : size] = edge
        for k in range(2):
            z[k, t, 0:SUB] = edge
            z[k, t, size - SUB : size] = edge
    chain((size - 2 * SUB - 2 * rows) // 2, outs, rows, scratch)


def wide_chain(slices, spread, coarse):
    tiles, both, _ = coarse.shape
    rows = both // 2
    bands = lax.axis_size("space")
    total = bands * rows
    length = spread.shape[1]
    every = lax.all_gather(spread, "space")
    gap = jnp.zeros((tiles, total, LANES), jnp.float32)
    for b in range(bands):
        at = (b * rows - SPILL + jnp.arange(length)) % total
        gap = gap.at[:, at].add(every[b])
    every = lax.all_gather(coarse, "space")
    old, psi = (jnp.moveaxis(every[:, :, k * rows : (k + 1) * rows], 0, 1).reshape(tiles, total, LANES) for k in range(2))
    pads = STAGES * slices
    first = lax.axis_index("space") // 2 * 2 * rows
    at = (first - pads + jnp.arange(2 * rows + 2 * pads)) % total
    size = 2 * rows + 2 * pads + 2 * SUB
    return pl.pallas_call(
        functools.partial(wide_chain_kernel, slices, rows),
        out_shape=(jax.ShapeDtypeStruct((tiles, rows, LANES), jnp.float32),) * slices,
        in_specs=[VMEM] * 3,
        out_specs=(VMEM,) * slices,
        scratch_shapes=chain_scratch(tiles, size, slices, rows),
        compiler_params=COMPACT,
        name="coarse",
    )(*(jnp.take(x, at, axis=1) for x in (gap, old, psi)))


def out_kernel(slices, fine, from_low, from_high, own, *refs):
    received, (out, tall) = refs[: slices - 1], refs[slices - 1 :]
    tiles, rows, _ = fine.shape
    count = rows // BLOCK
    n = lax.axis_index("cuts")
    lane = lane_index((count, LANES))
    per = LANES // BLOCK
    sources = [(n ^ k) if slices & (slices - 1) == 0 else lax.rem(n + slices - k, slices) for k in range(1, slices)]
    for k in range(tiles // BLOCK):
        total = own[k]
        for source, x in zip(sources, received, strict=True):
            total = total + jnp.where(source < n, x[k], 0.0)
        for q in range(BLOCK):
            t = k * BLOCK + q
            up = jnp.take_along_axis(total, q * per + lane // BLOCK, axis=1)
            for i in range(BLOCK):
                tall[t, pl.ds(i, count, stride=BLOCK)] = up
    for t in range(tiles):
        at = slice(t * LANES, (t + 1) * LANES)
        out[0, 0:REACH, at] = (fine[t, 0:REACH] + from_low[t]) + tall[t, 0:REACH]
        out[0, REACH : rows - REACH, at] = fine[t, REACH : rows - REACH] + tall[t, REACH : rows - REACH]
        out[0, rows - REACH : rows, at] = (fine[t, rows - REACH : rows] + from_high[t]) + tall[t, rows - REACH : rows]


def out_call(slices, fine, from_low, from_high, own, received):
    tiles, rows, _ = fine.shape
    return pl.pallas_call(
        functools.partial(out_kernel, slices),
        out_shape=jax.ShapeDtypeStruct((1, rows, tiles * LANES), jnp.float32),
        in_specs=[VMEM] * (3 + slices),
        out_specs=VMEM,
        scratch_shapes=[pltpu.VMEM((tiles, rows, LANES), jnp.float32)],
        compiler_params=COMPACT,
        name="total",
    )(fine, from_low, from_high, own, *received)


def per_device(states, stream):
    state = states[0]
    slices, bands = lax.axis_size("cuts"), lax.axis_size("space")
    rows = state.shape[0] // BLOCK
    up = [(i, (i + 1) % bands) for i in range(bands)]
    down = [(i, (i - 1) % bands) for i in range(bands)]
    twin = [(i, i ^ 1) for i in range(bands)]
    across = [(i, (i + 1 if i % 2 else i - 1) % bands) for i in range(bands)]

    def exchange(x, pairs):
        return lax.ppermute(x, "space", pairs)

    low = exchange(jnp.concatenate([state[-REACH:], stream[-REACH:]]), up)
    high = exchange(jnp.concatenate([state[:REACH], stream[:REACH]]), down)
    coarse = pre_call(state, stream)
    paired = bands % 2 == 0 and STAGES * (slices - 1) <= 2 * rows - SPILL
    if paired:
        coarse = pair_call(coarse, exchange(coarse, twin))
        coarse_near = exchange(coarse, across)
        coarse_far = exchange(coarse_near, twin)
    fine, edge_low, edge_high, spread = fine_call(state, stream, low, high)
    if paired:
        whole, message = spread_call(spread, exchange(spread, twin), rows)
        near = exchange(message, across)
        far = exchange(near, twin)
        from_low, from_high = exchange(edge_high, up), exchange(edge_low, down)
        *sent, own = pair_chain_call(slices, whole, near, far, coarse, coarse_near, coarse_far)
    else:
        from_low, from_high = exchange(edge_high, up), exchange(edge_low, down)
        *sent, own = wide_chain(slices, spread, coarse)
    received = [
        lax.ppermute(x, "cuts", [(i, partner(i, k, slices)) for i in range(slices)]) for k, x in enumerate(sent, 1)
    ]
    return out_call(slices, fine, from_low, from_high, own, received)


def solution(mesh):
    return jax.shard_map(
        per_device,
        mesh=mesh,
        in_specs=(P("cuts", "space", None), P("space", None)),
        out_specs=P("cuts", "space", None),
        check_vma=False,
    )
```

```python
import functools

import jax
import jax.numpy as jnp
from jax import lax
from jax.experimental import pallas as pl
from jax.experimental.pallas import tpu as pltpu
from jax.sharding import PartitionSpec as P

FINE_STEPS = 4
VISCOSITY = 0.2
FINE_DT = 0.25
BLOCK = 4
LANES = 128
SUB = 8
STAGES = 4
REACH = FINE_STEPS * STAGES // 2
SPILL = REACH // BLOCK
VMEM = pl.BlockSpec(memory_space=pltpu.VMEM)
COMPACT = pltpu.CompilerParams(vmem_limit_bytes=12 * 2**20)


def lane_index(shape):
    return lax.broadcasted_iota(jnp.int32, shape, len(shape) - 1)


def horner(diffusion):
    c = 4.0 * diffusion
    b = 24.0**-0.25
    powers = (
        1 - c + c**2 / 2 - c**3 / 6 + c**4 / 24,
        1 - c + c**2 / 2 - c**3 / 6,
        (1 - c + c**2 / 2) / 2,
        (1 - c) / 6,
    )
    return b, [powers[k] / b**k for k in (3, 2, 1, 0)]


def neighbours(source, rows, group):
    tiles = source.shape[0]
    lo, hi = rows
    lane = lane_index((hi - lo, LANES))
    first, last = lane == 0, lane == LANES - 1
    groups = tiles // group

    def eastern(k):
        return pltpu.roll(source[k % groups * group, lo:hi], LANES - 1, 1)

    east_here, west_before = eastern(0), pltpu.roll(source[tiles - 1, lo:hi], 1, 1)
    for k in range(groups):
        east_after = eastern(k + 1)
        here = [source[k * group + i, lo:hi] for i in range(group)]
        west_here = pltpu.roll(here[-1], 1, 1)
        for i in range(group):
            east = here[i + 1] if i + 1 < group else jnp.where(last, east_after, east_here)
            west = here[i - 1] if i else jnp.where(first, west_before, west_here)
            yield k * group + i, east, west
        east_here, west_before = east_after, west_here


def set_coefs(psi, coefs, rows, scale, diffusion, group):
    lo, hi = rows
    b, _ = horner(diffusion)
    scale, diffusion = scale * b, diffusion * b
    for t, east, west in neighbours(psi, rows, group):
        u = scale * (psi[t, lo + 1 : hi + 1] - psi[t, lo - 1 : hi - 1])
        v = scale * (west - east)
        coefs[0, t, lo:hi] = diffusion - u
        coefs[1, t, lo:hi] = diffusion + u
        coefs[2, t, lo:hi] = diffusion - v
        coefs[3, t, lo:hi] = diffusion + v


def stage(source, a, out, coefs, rows, factor, group):
    lo, hi = rows
    for t, east, west in neighbours(source, rows, group):
        along = coefs[0, t, lo:hi] * east + coefs[1, t, lo:hi] * west
        across = coefs[2, t, lo:hi] * source[t, lo + 1 : hi + 1] + coefs[3, t, lo:hi] * source[t, lo - 1 : hi - 1]
        out[t, lo:hi] = (along + across) + factor * a[t, lo:hi]


def step(a, z, coefs, rows, diffusion, group):
    _, factors = horner(diffusion)
    for k in range(STAGES):
        source = a if k == 0 else z.at[(k - 1) % 2]
        stage(source, a, a if k == STAGES - 1 else z.at[k % 2], coefs, rows[k], factors[k], group)


def transposed(parts):
    lane = lane_index(parts[0].shape)
    for width in (LANES // 4, LANES // 2):
        keep = lane // width % 2 == 0
        apart = 4 * width // LANES
        out = list(parts)
        for i in range(4):
            if i & apart == 0:
                j = i + apart
                out[i] = jnp.where(keep, parts[i], pltpu.roll(parts[j], width, 1))
                out[j] = jnp.where(keep, pltpu.roll(parts[i], LANES - width, 1), parts[j])
        parts = out
    return parts


def interleaved(parts):
    lane = lane_index(parts[0].shape)
    at = lane % (LANES // BLOCK) * BLOCK + lane // (LANES // BLOCK)
    return transposed([jnp.take_along_axis(x, at, axis=1) for x in parts])


def in_order(parts):
    lane = lane_index(parts[0].shape)
    at = lane % BLOCK * (LANES // BLOCK) + lane // BLOCK
    return [jnp.take_along_axis(x, at, axis=1) for x in transposed(parts)]


def spread_tiles(source, rows, put):
    lo, hi = rows
    for k in range(0, source.shape[1] // LANES, BLOCK):
        parts = [source[lo:hi, (k + i) * LANES : (k + i + 1) * LANES] for i in range(BLOCK)]
        for i, x in enumerate(interleaved(parts)):
            put(k + i, x)


def pooled(take, tiles, put):
    for k in range(tiles // BLOCK):
        sums = [(take(t, 0) + take(t, 1)) + (take(t, 2) + take(t, 3)) for t in range(k * BLOCK, (k + 1) * BLOCK)]
        put(k, ((sums[0] + sums[1]) + (sums[2] + sums[3])) * (1.0 / (BLOCK * BLOCK)))


def pre_kernel(states, stream, out, *tall):
    rows, cols = states.shape
    count = rows // BLOCK
    for k, source in enumerate((states, stream)):

        def keep(t, value, k=k):
            tall[k][t] = value

        def take(t, i, k=k):
            return tall[k][t, pl.ds(i, count, stride=BLOCK)]

        def put(t, value, k=k):
            out[t, k * count : (k + 1) * count] = value

        spread_tiles(source, (0, rows), keep)
        pooled(take, cols // LANES, put)


def pre_call(states, stream):
    rows, cols = states.shape
    tiles = cols // LANES
    tall = jax.ShapeDtypeStruct((tiles, rows, LANES), jnp.float32)
    return pl.pallas_call(
        pre_kernel,
        out_shape=(jax.ShapeDtypeStruct((tiles // BLOCK, 2 * rows // BLOCK, LANES), jnp.float32), tall, tall),
        in_specs=[VMEM] * 2,
        out_specs=(VMEM,) * 3,
        compiler_params=COMPACT,
        name="restrict",
    )(states, stream)


def fine_kernel(states, stream, low, high, fine, edge_low, edge_high, e_out, a, psi, z, coefs):
    tiles, rows, _ = states.shape
    own = SUB + REACH
    top = own + rows
    size = a.shape[1]
    for k, (buffer, source) in enumerate(((a, states), (psi, stream))):

        def below(t, value, buffer=buffer):
            buffer[t, SUB:own] = value

        def above(t, value, buffer=buffer):
            buffer[t, top : top + REACH] = value

        spread_tiles(low, (k * REACH, (k + 1) * REACH), below)
        spread_tiles(high, (k * REACH, (k + 1) * REACH), above)
        for t in range(tiles):
            buffer[t, own:top] = source[t]
    for t in range(tiles):
        for buffer in (a, psi, z.at[0], z.at[1]):
            buffer[t, 0:SUB] = jnp.zeros((SUB, LANES), jnp.float32)
            buffer[t, top + REACH : size] = jnp.zeros((size - top - REACH, LANES), jnp.float32)
    diffusion = VISCOSITY * FINE_DT
    group = BLOCK
    set_coefs(psi, coefs, (SUB, top + REACH), FINE_DT * 0.25, diffusion, group)

    def rows_at(n):
        reach = REACH - n if n <= REACH else n - REACH
        spare = -(rows + 2 * reach) % SUB
        reach += min(spare // 2, REACH - reach)
        return (own - reach, top + reach)

    half = FINE_STEPS // 2
    for n in range(half):
        step(a, z, coefs, [rows_at(n * STAGES + k) for k in range(1, STAGES + 1)], diffusion, group)
    nothing = jnp.zeros((REACH, LANES), jnp.float32)
    for t in range(tiles):
        for buffer in (a, z.at[0], z.at[1]):
            buffer[t, SUB:own] = nothing
            buffer[t, top : top + REACH] = nothing
    for n in range(half, FINE_STEPS):
        step(a, z, coefs, [rows_at(n * STAGES + k) for k in range(1, STAGES + 1)], diffusion, group)
    for t in range(tiles):
        fine[t] = a[t, own:top]
        edge_low[t] = a[t, SUB:own]
        edge_high[t] = a[t, top : top + REACH]
    spread = e_out.shape[1]

    def take(t, i):
        return a[t, pl.ds(SUB + i, spread, stride=BLOCK)]

    def put(k, value):
        e_out[k] = value

    pooled(take, tiles, put)


def fine_call(states, stream, low, high):
    tiles, rows, _ = states.shape
    spread = -(-(rows // BLOCK + 2 * SPILL) // SUB) * SUB
    size = SUB + max(BLOCK * spread, rows + 2 * REACH + SUB)
    f32 = jnp.float32
    return pl.pallas_call(
        fine_kernel,
        out_shape=(
            jax.ShapeDtypeStruct((tiles, rows, LANES), f32),
            jax.ShapeDtypeStruct((tiles, REACH, LANES), f32),
            jax.ShapeDtypeStruct((tiles, REACH, LANES), f32),
            jax.ShapeDtypeStruct((tiles // BLOCK, spread, LANES), f32),
        ),
        in_specs=[VMEM] * 4,
        out_specs=(VMEM,) * 4,
        scratch_shapes=[
            pltpu.VMEM((tiles, size, LANES), f32),
            pltpu.VMEM((tiles, size, LANES), f32),
            pltpu.VMEM((2, tiles, size, LANES), f32),
            pltpu.VMEM((4, tiles, size, LANES), f32),
        ],
        compiler_params=COMPACT,
        name="fine",
    )(states, stream, low, high)


def pair_kernel(mine, theirs, out):
    tiles, both, _ = mine.shape
    rows = both // 2
    odd = lax.rem(lax.axis_index("space"), 2) == 1
    for t in range(tiles):
        lower = jnp.where(odd, theirs[t], mine[t])
        upper = jnp.where(odd, mine[t], theirs[t])
        for k in range(2):
            out[t, 2 * k * rows : (2 * k + 1) * rows] = lower[k * rows : (k + 1) * rows]
            out[t, (2 * k + 1) * rows : (2 * k + 2) * rows] = upper[k * rows : (k + 1) * rows]


def pair_call(mine, theirs):
    tiles, both, _ = mine.shape
    return pl.pallas_call(
        pair_kernel,
        out_shape=jax.ShapeDtypeStruct((tiles, 2 * both, LANES), jnp.float32),
        in_specs=[VMEM] * 2,
        out_specs=VMEM,
        compiler_params=COMPACT,
        name="pair",
    )(mine, theirs)


def spread_kernel(rows, mine, theirs, whole, message):
    tiles, spread, _ = mine.shape
    odd = lax.rem(lax.axis_index("space"), 2) == 1
    for t in range(tiles):
        lower = jnp.where(odd, theirs[t], mine[t])
        upper = jnp.where(odd, mine[t], theirs[t])
        whole[t, 0:spread] = lower
        whole[t, spread:] = jnp.zeros((whole.shape[1] - spread, LANES), jnp.float32)
        whole[t, rows : rows + spread] = whole[t, rows : rows + spread] + upper
        message[t] = jnp.where(odd, whole[t, 2 * SPILL : 2 * SPILL + 2 * rows], whole[t, 0 : 2 * rows])


def spread_call(mine, theirs, rows):
    tiles, spread, _ = mine.shape
    f32 = jnp.float32
    return pl.pallas_call(
        functools.partial(spread_kernel, rows),
        out_shape=(
            jax.ShapeDtypeStruct((tiles, rows + spread, LANES), f32),
            jax.ShapeDtypeStruct((tiles, 2 * rows, LANES), f32),
        ),
        in_specs=[VMEM] * 2,
        out_specs=(VMEM,) * 2,
        compiler_params=COMPACT,
        name="spread",
    )(mine, theirs)


def partner(n, k, size):
    return n ^ k if size & (size - 1) == 0 else (n + k) % size


def chain(pads, outs, rows, scratch):
    gap, old, psi, z, coefs, powers = scratch
    tiles, size, _ = gap.shape
    spacing, length = float(BLOCK), FINE_DT * FINE_STEPS
    diffusion = VISCOSITY * length / (spacing * spacing)
    whole = (SUB, size - SUB)
    base = SUB + pads
    slices = len(outs)
    own = base + pl.multiple_of(rows * lax.rem(lax.axis_index("space"), 2), SUB)
    group = 1
    set_coefs(psi, coefs, whole, length / (2.0 * spacing) / (2.0 * spacing), diffusion, group)
    step(old, z, coefs, [whole] * STAGES, diffusion, group)
    n = lax.axis_index("cuts")
    for t in range(tiles):
        start = jnp.where(n == 0, old[t, whole[0] : whole[1]], 0.0)
        gap[t, whole[0] : whole[1]] = (gap[t, whole[0] : whole[1]] - old[t, whole[0] : whole[1]]) + start
        mine = old[t, pl.ds(own, rows)]
        outs[-1][t] = jnp.where(n == 0, mine, 0.0) - mine
    reach = STAGES * (slices - 1)

    def around(extent):
        extent = min(-(-extent // SUB) * SUB, pads)
        return (base - extent, base + 2 * rows + extent)

    for j in range(1, slices):
        reach -= STAGES
        step(gap, z, coefs, [around(reach + STAGES - k) for k in range(1, STAGES + 1)], diffusion, group)
        for t in range(tiles):
            powers[j, t] = gap[t, pl.ds(own, rows)]
    for k in range(1, slices):
        ahead = jnp.clip(partner(n, k, slices) - n, 1, slices - 1)
        for t in range(tiles):
            outs[k - 1][t] = powers[ahead, t]


def pair_chain_kernel(slices, rows, whole, message, passed, coarse, coarse_near, coarse_far, *refs):
    outs, scratch = refs[:slices], refs[slices:]
    gap, old, psi, z = scratch[:4]
    tiles = gap.shape[0]
    size = gap.shape[1]
    odd = lax.rem(lax.axis_index("space"), 2) == 1
    pads = 2 * rows
    base = SUB + pads
    edge = jnp.zeros((SUB, LANES), jnp.float32)
    for t in range(tiles):
        before, after = jnp.where(odd, passed[t], message[t]), jnp.where(odd, message[t], passed[t])
        gap[t] = jnp.zeros((size, LANES), jnp.float32)
        at = base - SPILL
        gap[t, at : at + whole.shape[1]] = whole[t]
        at = base + SPILL - 2 * rows
        gap[t, at : at + 2 * rows] = gap[t, at : at + 2 * rows] + before
        at = base - SPILL + 2 * rows
        gap[t, at : at + 2 * rows] = gap[t, at : at + 2 * rows] + after
        before = jnp.where(odd, coarse_far[t], coarse_near[t])
        after = jnp.where(odd, coarse_near[t], coarse_far[t])
        for k, out in ((0, old), (1, psi)):
            part = slice(2 * k * rows, 2 * (k + 1) * rows)
            out[t, 0:SUB] = edge
            out[t, SUB:base] = before[part]
            out[t, base : base + 2 * rows] = coarse[t, part]
            out[t, base + 2 * rows : base + 4 * rows] = after[part]
            out[t, size - SUB : size] = edge
        for k in range(2):
            z[k, t, 0:SUB] = edge
            z[k, t, size - SUB : size] = edge
    chain(pads, outs, rows, scratch)


def chain_scratch(tiles, size, slices, rows):
    f32 = jnp.float32
    return [
        pltpu.VMEM((tiles, size, LANES), f32),
        pltpu.VMEM((tiles, size, LANES), f32),
        pltpu.VMEM((tiles, size, LANES), f32),
        pltpu.VMEM((2, tiles, size, LANES), f32),
        pltpu.VMEM((4, tiles, size, LANES), f32),
        pltpu.VMEM((slices, tiles, rows, LANES), f32),
    ]


def pair_chain_call(slices, whole, message, passed, coarse, coarse_near, coarse_far):
    tiles = whole.shape[0]
    rows = message.shape[1] // 2
    return pl.pallas_call(
        functools.partial(pair_chain_kernel, slices, rows),
        out_shape=(jax.ShapeDtypeStruct((tiles, rows, LANES), jnp.float32),) * slices,
        in_specs=[VMEM] * 6,
        out_specs=(VMEM,) * slices,
        scratch_shapes=chain_scratch(tiles, 6 * rows + 2 * SUB, slices, rows),
        compiler_params=COMPACT,
        name="coarse",
    )(whole, message, passed, coarse, coarse_near, coarse_far)


def wide_chain_kernel(slices, rows, gap_in, old_in, psi_in, *refs):
    outs, scratch = refs[:slices], refs[slices:]
    gap, old, psi, z = scratch[:4]
    tiles, size, _ = gap.shape
    edge = jnp.zeros((SUB, LANES), jnp.float32)
    for t in range(tiles):
        for source, out in ((gap_in, gap), (old_in, old), (psi_in, psi)):
            out[t, 0:SUB] = edge
            out[t, SUB : size - SUB] = source[t]
            out[t, size - SUB : size] = edge
        for k in range(2):
            z[k, t, 0:SUB] = edge
            z[k, t, size - SUB : size] = edge
    chain((size - 2 * SUB - 2 * rows) // 2, outs, rows, scratch)


def wide_chain(slices, spread, coarse):
    tiles, both, _ = coarse.shape
    rows = both // 2
    bands = lax.axis_size("space")
    total = bands * rows
    length = spread.shape[1]
    every = lax.all_gather(spread, "space")
    gap = jnp.zeros((tiles, total, LANES), jnp.float32)
    for b in range(bands):
        at = (b * rows - SPILL + jnp.arange(length)) % total
        gap = gap.at[:, at].add(every[b])
    every = lax.all_gather(coarse, "space")
    old, psi = (jnp.moveaxis(every[:, :, k * rows : (k + 1) * rows], 0, 1).reshape(tiles, total, LANES) for k in range(2))
    pads = STAGES * slices
    first = lax.axis_index("space") // 2 * 2 * rows
    at = (first - pads + jnp.arange(2 * rows + 2 * pads)) % total
    size = 2 * rows + 2 * pads + 2 * SUB
    return pl.pallas_call(
        functools.partial(wide_chain_kernel, slices, rows),
        out_shape=(jax.ShapeDtypeStruct((tiles, rows, LANES), jnp.float32),) * slices,
        in_specs=[VMEM] * 3,
        out_specs=(VMEM,) * slices,
        scratch_shapes=chain_scratch(tiles, size, slices, rows),
        compiler_params=COMPACT,
        name="coarse",
    )(*(jnp.take(x, at, axis=1) for x in (gap, old, psi)))


def settle_kernel(fine, from_low, from_high, out, tall):
    tiles, rows, _ = fine.shape
    for t in range(tiles):
        tall[t, 0:REACH] = fine[t, 0:REACH] + from_low[t]
        tall[t, REACH : rows - REACH] = fine[t, REACH : rows - REACH]
        tall[t, rows - REACH : rows] = fine[t, rows - REACH : rows] + from_high[t]
    for k in range(0, tiles, BLOCK):
        for i, x in enumerate(in_order([tall[k + i] for i in range(BLOCK)])):
            out[:, (k + i) * LANES : (k + i + 1) * LANES] = x


def settle_call(fine, from_low, from_high):
    tiles, rows, _ = fine.shape
    return pl.pallas_call(
        settle_kernel,
        out_shape=jax.ShapeDtypeStruct((rows, tiles * LANES), jnp.float32),
        in_specs=[VMEM] * 3,
        out_specs=VMEM,
        scratch_shapes=[pltpu.VMEM((tiles, rows, LANES), jnp.float32)],
        compiler_params=COMPACT,
        name="settle",
    )(fine, from_low, from_high)


def out_kernel(slices, fine, own, *refs):
    received, (out, tall) = refs[: slices - 1], refs[slices - 1 :]
    rows, cols = fine.shape
    count = rows // BLOCK
    n = lax.axis_index("cuts")
    lane = lane_index((count, LANES))
    per = LANES // BLOCK
    sources = [(n ^ k) if slices & (slices - 1) == 0 else lax.rem(n + slices - k, slices) for k in range(1, slices)]
    for k in range(cols // LANES // BLOCK):
        total = own[k]
        for source, x in zip(sources, received, strict=True):
            total = total + jnp.where(source < n, x[k], 0.0)
        for q in range(BLOCK):
            t = k * BLOCK + q
            up = jnp.take_along_axis(total, q * per + lane // BLOCK, axis=1)
            for i in range(BLOCK):
                tall[t, pl.ds(i, count, stride=BLOCK)] = up
            at = slice(t * LANES, (t + 1) * LANES)
            out[0, :, at] = fine[:, at] + tall[t]


def out_call(slices, fine, own, received):
    rows, cols = fine.shape
    return pl.pallas_call(
        functools.partial(out_kernel, slices),
        out_shape=jax.ShapeDtypeStruct((1, rows, cols), jnp.float32),
        in_specs=[VMEM] * (1 + slices),
        out_specs=VMEM,
        scratch_shapes=[pltpu.VMEM((cols // LANES, rows, LANES), jnp.float32)],
        compiler_params=COMPACT,
        name="total",
    )(fine, own, *received)


def iteration(states, stream):
    state = states[0]
    slices, bands = lax.axis_size("cuts"), lax.axis_size("space")
    rows = state.shape[0] // BLOCK
    up = [(i, (i + 1) % bands) for i in range(bands)]
    down = [(i, (i - 1) % bands) for i in range(bands)]
    twin = [(i, i ^ 1) for i in range(bands)]
    across = [(i, (i + 1 if i % 2 else i - 1) % bands) for i in range(bands)]

    def exchange(x, pairs):
        return lax.ppermute(x, "space", pairs)

    low = exchange(jnp.concatenate([state[-REACH:], stream[-REACH:]]), up)
    high = exchange(jnp.concatenate([state[:REACH], stream[:REACH]]), down)
    coarse, state, stream = pre_call(state, stream)
    paired = bands % 2 == 0 and STAGES * (slices - 1) <= 2 * rows - SPILL
    if paired:
        coarse = pair_call(coarse, exchange(coarse, twin))
        coarse_near = exchange(coarse, across)
        coarse_far = exchange(coarse_near, twin)
    fine, edge_low, edge_high, spread = fine_call(state, stream, low, high)
    if paired:
        whole, message = spread_call(spread, exchange(spread, twin), rows)
        near = exchange(message, across)
        far = exchange(near, twin)
        from_low, from_high = exchange(edge_high, up), exchange(edge_low, down)
        *sent, own = pair_chain_call(slices, whole, near, far, coarse, coarse_near, coarse_far)
    else:
        from_low, from_high = exchange(edge_high, up), exchange(edge_low, down)
        *sent, own = wide_chain(slices, spread, coarse)
    received = []
    for k, x in enumerate(sent, 1):
        received.append(lax.ppermute(x, "cuts", [(i, partner(i, k, slices)) for i in range(slices)]))
    return out_call(slices, settle_call(fine, from_low, from_high), own, received)


def solution(mesh):
    return jax.shard_map(
        iteration,
        mesh=mesh,
        in_specs=(P("cuts", "space", None), P("space", None)),
        out_specs=P("cuts", "space", None),
        check_vma=False,
    )
```

```python
import functools

import jax
import jax.numpy as jnp
from jax import lax
from jax.experimental import pallas as pl
from jax.experimental.pallas import tpu as pltpu
from jax.sharding import PartitionSpec as P

FINE_STEPS = 4
VISCOSITY = 0.2
FINE_DT = 0.25
BLOCK = 4
LANES = 128
SUB = 8
STAGES = 4
REACH = FINE_STEPS * STAGES // 2
SPILL = REACH // BLOCK
VMEM = pl.BlockSpec(memory_space=pltpu.VMEM)
COMPACT = pltpu.CompilerParams(vmem_limit_bytes=12 * 2**20)


def lane_index(shape):
    return lax.broadcasted_iota(jnp.int32, shape, len(shape) - 1)


def horner(diffusion):
    c = 4.0 * diffusion
    b = 24.0**-0.25
    powers = (
        1 - c + c**2 / 2 - c**3 / 6 + c**4 / 24,
        1 - c + c**2 / 2 - c**3 / 6,
        (1 - c + c**2 / 2) / 2,
        (1 - c) / 6,
    )
    return b, [powers[k] / b**k for k in (3, 2, 1, 0)]


def neighbours(source, rows, group):
    tiles = source.shape[0]
    lo, hi = rows
    lane = lane_index((hi - lo, LANES))
    first, last = lane == 0, lane == LANES - 1
    groups = tiles // group

    def eastern(k):
        return pltpu.roll(source[k % groups * group, lo:hi], LANES - 1, 1)

    east_here, west_before = eastern(0), pltpu.roll(source[tiles - 1, lo:hi], 1, 1)
    for k in range(groups):
        east_after = eastern(k + 1)
        here = [source[k * group + i, lo:hi] for i in range(group)]
        west_here = pltpu.roll(here[-1], 1, 1)
        for i in range(group):
            east = here[i + 1] if i + 1 < group else jnp.where(last, east_after, east_here)
            west = here[i - 1] if i else jnp.where(first, west_before, west_here)
            yield k * group + i, east, west
        east_here, west_before = east_after, west_here


def set_coefs(psi, coefs, rows, scale, diffusion, group):
    lo, hi = rows
    b, _ = horner(diffusion)
    scale, diffusion = scale * b, diffusion * b
    for t, east, west in neighbours(psi, rows, group):
        u = scale * (psi[t, lo + 1 : hi + 1] - psi[t, lo - 1 : hi - 1])
        v = scale * (west - east)
        coefs[0, t, lo:hi] = diffusion - u
        coefs[1, t, lo:hi] = diffusion + u
        coefs[2, t, lo:hi] = diffusion - v
        coefs[3, t, lo:hi] = diffusion + v


def stage(source, a, out, coefs, rows, factor, group):
    lo, hi = rows
    for t, east, west in neighbours(source, rows, group):
        along = coefs[0, t, lo:hi] * east + coefs[1, t, lo:hi] * west
        across = coefs[2, t, lo:hi] * source[t, lo + 1 : hi + 1] + coefs[3, t, lo:hi] * source[t, lo - 1 : hi - 1]
        out[t, lo:hi] = (along + across) + factor * a[t, lo:hi]


def step(a, z, coefs, rows, diffusion, group):
    _, factors = horner(diffusion)
    for k in range(STAGES):
        source = a if k == 0 else z.at[(k - 1) % 2]
        stage(source, a, a if k == STAGES - 1 else z.at[k % 2], coefs, rows[k], factors[k], group)


def transposed(parts):
    lane = lane_index(parts[0].shape)
    for width in (LANES // 4, LANES // 2):
        keep = lane // width % 2 == 0
        apart = 4 * width // LANES
        out = list(parts)
        for i in range(4):
            if i & apart == 0:
                j = i + apart
                out[i] = jnp.where(keep, parts[i], pltpu.roll(parts[j], width, 1))
                out[j] = jnp.where(keep, pltpu.roll(parts[i], LANES - width, 1), parts[j])
        parts = out
    return parts


def interleaved(parts):
    lane = lane_index(parts[0].shape)
    at = lane % (LANES // BLOCK) * BLOCK + lane // (LANES // BLOCK)
    return transposed([jnp.take_along_axis(x, at, axis=1) for x in parts])


def in_order(parts):
    lane = lane_index(parts[0].shape)
    at = lane % BLOCK * (LANES // BLOCK) + lane // BLOCK
    return [jnp.take_along_axis(x, at, axis=1) for x in transposed(parts)]


def spread_tiles(source, rows, put):
    lo, hi = rows
    for k in range(0, source.shape[1] // LANES, BLOCK):
        parts = [source[lo:hi, (k + i) * LANES : (k + i + 1) * LANES] for i in range(BLOCK)]
        for i, x in enumerate(interleaved(parts)):
            put(k + i, x)


def pooled(take, tiles, put):
    for k in range(tiles // BLOCK):
        sums = [(take(t, 0) + take(t, 1)) + (take(t, 2) + take(t, 3)) for t in range(k * BLOCK, (k + 1) * BLOCK)]
        put(k, ((sums[0] + sums[1]) + (sums[2] + sums[3])) * (1.0 / (BLOCK * BLOCK)))


def rows_kernel(states, stream, to_next, to_previous, sems):
    rows = states.shape[0]
    copies = [
        pltpu.make_async_copy(
            source.at[pl.ds(first, REACH)], out.at[pl.ds(k * REACH, REACH)], sems.at[2 * j + k]
        )
        for j, (out, first) in enumerate(((to_next, rows - REACH), (to_previous, 0)))
        for k, source in enumerate((states, stream))
    ]
    for copy in copies:
        copy.start()
    for copy in copies:
        copy.wait()


def rows_call(states, stream):
    out = jax.ShapeDtypeStruct((2 * REACH, states.shape[1]), jnp.float32)
    return pl.pallas_call(
        rows_kernel,
        out_shape=(out, out),
        in_specs=[pl.BlockSpec(memory_space=pltpu.HBM)] * 2,
        out_specs=(VMEM,) * 2,
        scratch_shapes=[pltpu.SemaphoreType.DMA((4,))],
        compiler_params=COMPACT,
        name="rows",
    )(*(pltpu.with_memory_space_constraint(x, pltpu.HBM) for x in (states, stream)))


def restrict_kernel(states, stream, out, tall):
    rows, cols = states.shape
    count = rows // BLOCK
    lane = lane_index((count, LANES))
    per = LANES // BLOCK
    for k, source in enumerate((states, stream)):
        for t in range(cols // LANES):
            tall[k, t] = source[:, t * LANES : (t + 1) * LANES]
        for c in range(cols // LANES // BLOCK):
            whole = jnp.zeros((count, LANES), jnp.float32)
            for q in range(BLOCK):
                part = [tall[k, c * BLOCK + q, pl.ds(i, count, stride=BLOCK)] for i in range(BLOCK)]
                x = (part[0] + part[1]) + (part[2] + part[3])
                x = x + pltpu.roll(x, LANES - 1, 1)
                x = x + pltpu.roll(x, LANES - 2, 1)
                x = jnp.take_along_axis(x, lane * BLOCK % LANES, axis=1)
                whole = jnp.where(lane // per == q, x, whole)
            out[c, k * count : (k + 1) * count] = whole * (1.0 / (BLOCK * BLOCK))


def restrict_call(states, stream):
    rows, cols = states.shape
    tiles = cols // LANES
    return pl.pallas_call(
        restrict_kernel,
        out_shape=jax.ShapeDtypeStruct((tiles // BLOCK, 2 * rows // BLOCK, LANES), jnp.float32),
        in_specs=[VMEM] * 2,
        out_specs=VMEM,
        scratch_shapes=[pltpu.VMEM((2, tiles, rows, LANES), jnp.float32)],
        compiler_params=COMPACT,
        name="restrict",
    )(states, stream)


def interleave_kernel(states, stream, *tall):
    for source, out in zip((states, stream), tall, strict=True):

        def keep(t, value, out=out):
            out[t] = value

        spread_tiles(source, (0, source.shape[0]), keep)


def interleave_call(states, stream):
    rows, cols = states.shape
    tall = jax.ShapeDtypeStruct((cols // LANES, rows, LANES), jnp.float32)
    return pl.pallas_call(
        interleave_kernel,
        out_shape=(tall, tall),
        in_specs=[VMEM] * 2,
        out_specs=(VMEM,) * 2,
        compiler_params=COMPACT,
        name="interleave",
    )(states, stream)


def fine_kernel(states, stream, low, high, fine, edge_twin, edge_across, e_out, a, psi, z, coefs):
    odd = band_of_pair() == 1
    tiles, rows, _ = states.shape
    own = SUB + REACH
    top = own + rows
    size = a.shape[1]
    for k, (buffer, source) in enumerate(((a, states), (psi, stream))):

        def below(t, value, buffer=buffer):
            buffer[t, SUB:own] = value

        def above(t, value, buffer=buffer):
            buffer[t, top : top + REACH] = value

        spread_tiles(low, (k * REACH, (k + 1) * REACH), below)
        spread_tiles(high, (k * REACH, (k + 1) * REACH), above)
        for t in range(tiles):
            buffer[t, own:top] = source[t]
    for t in range(tiles):
        for buffer in (a, psi, z.at[0], z.at[1]):
            buffer[t, 0:SUB] = jnp.zeros((SUB, LANES), jnp.float32)
            buffer[t, top + REACH : size] = jnp.zeros((size - top - REACH, LANES), jnp.float32)
    diffusion = VISCOSITY * FINE_DT
    group = BLOCK
    set_coefs(psi, coefs, (SUB, top + REACH), FINE_DT * 0.25, diffusion, group)

    def rows_at(n):
        reach = REACH - n if n <= REACH else n - REACH
        spare = -(rows + 2 * reach) % SUB
        reach += min(spare // 2, REACH - reach)
        return (own - reach, top + reach)

    half = FINE_STEPS // 2
    for n in range(half):
        step(a, z, coefs, [rows_at(n * STAGES + k) for k in range(1, STAGES + 1)], diffusion, group)
    nothing = jnp.zeros((REACH, LANES), jnp.float32)
    for t in range(tiles):
        for buffer in (a, z.at[0], z.at[1]):
            buffer[t, SUB:own] = nothing
            buffer[t, top : top + REACH] = nothing
    for n in range(half, FINE_STEPS):
        step(a, z, coefs, [rows_at(n * STAGES + k) for k in range(1, STAGES + 1)], diffusion, group)
    for t in range(tiles):
        fine[t] = a[t, own:top]
        below, above = a[t, SUB:own], a[t, top : top + REACH]
        edge_twin[t] = jnp.where(odd, below, above)
        edge_across[t] = jnp.where(odd, above, below)
    spread = e_out.shape[1]

    def take(t, i):
        return a[t, pl.ds(SUB + i, spread, stride=BLOCK)]

    def put(k, value):
        e_out[k] = value

    pooled(take, tiles, put)


def fine_call(states, stream, low, high):
    tiles, rows, _ = states.shape
    spread = -(-(rows // BLOCK + 2 * SPILL) // SUB) * SUB
    size = SUB + max(BLOCK * spread, rows + 2 * REACH + SUB)
    f32 = jnp.float32
    return pl.pallas_call(
        fine_kernel,
        out_shape=(
            jax.ShapeDtypeStruct((tiles, rows, LANES), f32),
            jax.ShapeDtypeStruct((tiles, REACH, LANES), f32),
            jax.ShapeDtypeStruct((tiles, REACH, LANES), f32),
            jax.ShapeDtypeStruct((tiles // BLOCK, spread, LANES), f32),
        ),
        in_specs=[VMEM] * 4,
        out_specs=(VMEM,) * 4,
        scratch_shapes=[
            pltpu.VMEM((tiles, size, LANES), f32),
            pltpu.VMEM((tiles, size, LANES), f32),
            pltpu.VMEM((2, tiles, size, LANES), f32),
            pltpu.VMEM((4, tiles, size, LANES), f32),
        ],
        compiler_params=COMPACT,
        name="fine",
    )(states, stream, low, high)


def pair_kernel(mine, theirs, out):
    tiles, both, _ = mine.shape
    rows = both // 2
    odd = lax.rem(lax.axis_index("space"), 2) == 1
    for t in range(tiles):
        lower = jnp.where(odd, theirs[t], mine[t])
        upper = jnp.where(odd, mine[t], theirs[t])
        for k in range(2):
            out[t, 2 * k * rows : (2 * k + 1) * rows] = lower[k * rows : (k + 1) * rows]
            out[t, (2 * k + 1) * rows : (2 * k + 2) * rows] = upper[k * rows : (k + 1) * rows]


def pair_call(mine, theirs):
    tiles, both, _ = mine.shape
    return pl.pallas_call(
        pair_kernel,
        out_shape=jax.ShapeDtypeStruct((tiles, 2 * both, LANES), jnp.float32),
        in_specs=[VMEM] * 2,
        out_specs=VMEM,
        compiler_params=COMPACT,
        name="pair",
    )(mine, theirs)


def spread_kernel(rows, mine, theirs, whole, message):
    tiles, spread, _ = mine.shape
    odd = lax.rem(lax.axis_index("space"), 2) == 1
    for t in range(tiles):
        lower = jnp.where(odd, theirs[t], mine[t])
        upper = jnp.where(odd, mine[t], theirs[t])
        whole[t, 0:spread] = lower
        whole[t, spread:] = jnp.zeros((whole.shape[1] - spread, LANES), jnp.float32)
        whole[t, rows : rows + spread] = whole[t, rows : rows + spread] + upper
        message[t] = jnp.where(odd, whole[t, 2 * SPILL : 2 * SPILL + 2 * rows], whole[t, 0 : 2 * rows])


def spread_call(mine, theirs, rows):
    tiles, spread, _ = mine.shape
    f32 = jnp.float32
    return pl.pallas_call(
        functools.partial(spread_kernel, rows),
        out_shape=(
            jax.ShapeDtypeStruct((tiles, rows + spread, LANES), f32),
            jax.ShapeDtypeStruct((tiles, 2 * rows, LANES), f32),
        ),
        in_specs=[VMEM] * 2,
        out_specs=(VMEM,) * 2,
        compiler_params=COMPACT,
        name="spread",
    )(mine, theirs)


def partners(slices):
    if slices == 4:
        return [(2, 3, 1, 0), (3, 2, 0, 1), (1, 0, 3, 2)]
    return [tuple((i + k) % slices for i in range(slices)) for k in range(1, slices)]


def pick(n, table):
    return sum(jnp.where(n == i, x, 0) for i, x in enumerate(table))


def coarse_rows(reach, rows, pads):
    reach = min(reach + -(rows + 2 * reach) % SUB // 2, pads)
    return (SUB + pads - reach, SUB + pads + rows + reach)


def coarse_diffusion():
    return VISCOSITY * FINE_DT * FINE_STEPS / (BLOCK * BLOCK)


def prepare(psi, old, z, coefs, rows, pads, slices):
    step_size, spacing = FINE_DT * FINE_STEPS, float(BLOCK)
    diffusion = coarse_diffusion()
    set_coefs(psi, coefs, (SUB, SUB + rows + 2 * pads), step_size / (4.0 * spacing * spacing), diffusion, 1)
    reach = STAGES * slices
    step(old, z, coefs, [coarse_rows(reach - k, rows, pads) for k in range(1, STAGES + 1)], diffusion, 1)


def clear_edges(buffers):
    edge = jnp.zeros((SUB, LANES), jnp.float32)
    for buffer in buffers:
        for t in range(buffer.shape[0]):
            buffer[t, 0:SUB] = edge
            buffer[t, buffer.shape[1] - SUB :] = edge


def band_of_pair():
    return lax.rem(lax.axis_index("space"), 2)


def pair_prepare_kernel(slices, rows, pair, near, far, old, coefs, psi, z, wide):
    odd = band_of_pair() == 1
    pads = 2 * rows
    first = pl.multiple_of(rows * band_of_pair(), SUB)
    clear_edges((old, psi, z.at[0], z.at[1]))
    for k, out in enumerate((old, psi)):
        part = slice(2 * k * rows, 2 * (k + 1) * rows)
        for t in range(out.shape[0]):
            wide[t, 0:pads] = jnp.where(odd, far[t, part], near[t, part])
            wide[t, pads : 2 * pads] = pair[t, part]
            wide[t, 2 * pads : 3 * pads] = jnp.where(odd, near[t, part], far[t, part])
            out[t, SUB : SUB + rows + 2 * pads] = wide[t, pl.ds(first, rows + 2 * pads)]
    prepare(psi, old, z, coefs, rows, pads, slices)


def prepare_shapes(tiles, size):
    f32 = jnp.float32
    return (
        (jax.ShapeDtypeStruct((tiles, size, LANES), f32), jax.ShapeDtypeStruct((4, tiles, size, LANES), f32)),
        [pltpu.VMEM((tiles, size, LANES), f32), pltpu.VMEM((2, tiles, size, LANES), f32)],
    )


def pair_prepare_call(slices, pair, near, far):
    tiles, total, _ = pair.shape
    rows = total // 4
    shapes, scratch = prepare_shapes(tiles, 5 * rows + 2 * SUB)
    return pl.pallas_call(
        functools.partial(pair_prepare_kernel, slices, rows),
        out_shape=shapes,
        in_specs=[VMEM] * 3,
        out_specs=(VMEM,) * 2,
        scratch_shapes=scratch + [pltpu.VMEM((tiles, 6 * rows, LANES), jnp.float32)],
        compiler_params=COMPACT,
        name="prepare",
    )(pair, near, far)


def chain(gap, old, z, coefs, powers, outs, rows, pads):
    slices = len(outs)
    n = lax.axis_index("cuts")
    own = slice(SUB + pads, SUB + pads + rows)
    extent = slice(*coarse_rows(STAGES * (slices - 1), rows, pads))
    for t in range(gap.shape[0]):
        start = jnp.where(n == 0, old[t, extent], 0.0)
        gap[t, extent] = (gap[t, extent] - old[t, extent]) + start
        mine = old[t, own]
        outs[-1][t] = jnp.where(n == 0, mine, 0.0) - mine
    reach = STAGES * (slices - 1)
    for j in range(1, slices):
        step(gap, z, coefs, [coarse_rows(reach - k, rows, pads) for k in range(1, STAGES + 1)], coarse_diffusion(), 1)
        reach -= STAGES
        for t in range(gap.shape[0]):
            powers[j, t] = gap[t, own]
    for out, table in zip(outs[:-1], partners(slices), strict=True):
        ahead = pick(n, [max(x - i, 1) for i, x in enumerate(table)])
        for t in range(gap.shape[0]):
            out[t] = powers[ahead, t]


def pair_chain_kernel(slices, rows, whole, message, passed, old, coefs, *refs):
    outs, (gap, z, powers, wide) = refs[:slices], refs[slices:]
    odd = band_of_pair() == 1
    pads = 2 * rows
    first = pl.multiple_of(rows * band_of_pair(), SUB)
    clear_edges((gap, z.at[0], z.at[1]))
    for t in range(gap.shape[0]):
        wide[t] = jnp.zeros(wide.shape[1:], jnp.float32)
        at = pads - SPILL
        wide[t, at : at + whole.shape[1]] = whole[t]
        for at, x in (
            (pads + SPILL - 2 * rows, jnp.where(odd, passed[t], message[t])),
            (pads - SPILL + 2 * rows, jnp.where(odd, message[t], passed[t])),
        ):
            wide[t, at : at + 2 * rows] = wide[t, at : at + 2 * rows] + x
        gap[t, SUB : SUB + rows + 2 * pads] = wide[t, pl.ds(first, rows + 2 * pads)]
    chain(gap, old, z, coefs, powers, outs, rows, pads)


def chain_shapes(tiles, size, slices, rows):
    f32 = jnp.float32
    return (
        (jax.ShapeDtypeStruct((tiles, rows, LANES), f32),) * slices,
        [
            pltpu.VMEM((tiles, size, LANES), f32),
            pltpu.VMEM((2, tiles, size, LANES), f32),
            pltpu.VMEM((slices, tiles, rows, LANES), f32),
        ],
    )


def pair_chain_call(slices, whole, message, passed, old, coefs):
    tiles = whole.shape[0]
    rows = message.shape[1] // 2
    shapes, scratch = chain_shapes(tiles, old.shape[1], slices, rows)
    return pl.pallas_call(
        functools.partial(pair_chain_kernel, slices, rows),
        out_shape=shapes,
        in_specs=[VMEM] * 5,
        out_specs=(VMEM,) * slices,
        scratch_shapes=scratch + [pltpu.VMEM((tiles, 6 * rows, LANES), jnp.float32)],
        compiler_params=COMPACT,
        name="coarse",
    )(whole, message, passed, old, coefs)


def wide_chain_kernel(slices, rows, pads, gap_in, old_in, psi_in, *refs):
    outs, (gap, z, powers, old, coefs, psi) = refs[:slices], refs[slices:]
    clear_edges((gap, old, psi, z.at[0], z.at[1]))
    for source, out in ((gap_in, gap), (old_in, old), (psi_in, psi)):
        for t in range(gap.shape[0]):
            out[t, SUB : SUB + rows + 2 * pads] = source[t]
    prepare(psi, old, z, coefs, rows, pads, slices)
    chain(gap, old, z, coefs, powers, outs, rows, pads)


def wide_chain(slices, spread, coarse):
    tiles, both, _ = coarse.shape
    rows = both // 2
    bands = lax.axis_size("space")
    total = bands * rows
    length = spread.shape[1]
    every = lax.all_gather(spread, "space")
    gap = jnp.zeros((tiles, total, LANES), jnp.float32)
    for b in range(bands):
        at = (b * rows - SPILL + jnp.arange(length)) % total
        gap = gap.at[:, at].add(every[b])
    every = lax.all_gather(coarse, "space")
    old, psi = (jnp.moveaxis(every[:, :, k * rows : (k + 1) * rows], 0, 1).reshape(tiles, total, LANES) for k in range(2))
    pads = -(-STAGES * slices // SUB) * SUB
    at = (lax.axis_index("space") * rows - pads + jnp.arange(rows + 2 * pads)) % total
    size = rows + 2 * pads + 2 * SUB
    shapes, scratch = chain_shapes(tiles, size, slices, rows)
    more = [pltpu.VMEM(x.shape, x.dtype) for x in prepare_shapes(tiles, size)[0]]
    return pl.pallas_call(
        functools.partial(wide_chain_kernel, slices, rows, pads),
        out_shape=shapes,
        in_specs=[VMEM] * 3,
        out_specs=(VMEM,) * slices,
        scratch_shapes=scratch + more + [pltpu.VMEM((tiles, size, LANES), jnp.float32)],
        compiler_params=COMPACT,
        name="coarse",
    )(*(jnp.take(x, at, axis=1) for x in (gap, old, psi)))


def settle_kernel(fine, from_twin, from_across, out, tall):
    tiles, rows, _ = fine.shape
    odd = band_of_pair() == 1
    for t in range(tiles):
        tall[t, 0:REACH] = fine[t, 0:REACH] + jnp.where(odd, from_twin[t], from_across[t])
        tall[t, REACH : rows - REACH] = fine[t, REACH : rows - REACH]
        tall[t, rows - REACH : rows] = fine[t, rows - REACH : rows] + jnp.where(odd, from_across[t], from_twin[t])
    for k in range(0, tiles, BLOCK):
        for i, x in enumerate(in_order([tall[k + i] for i in range(BLOCK)])):
            out[:, (k + i) * LANES : (k + i + 1) * LANES] = x


def settle_call(fine, from_twin, from_across):
    tiles, rows, _ = fine.shape
    return pl.pallas_call(
        settle_kernel,
        out_shape=jax.ShapeDtypeStruct((rows, tiles * LANES), jnp.float32),
        in_specs=[VMEM] * 3,
        out_specs=VMEM,
        scratch_shapes=[pltpu.VMEM((tiles, rows, LANES), jnp.float32)],
        compiler_params=COMPACT,
        name="settle",
    )(fine, from_twin, from_across)


def out_kernel(slices, fine, own, *refs):
    received, (out, tall) = refs[: slices - 1], refs[slices - 1 :]
    rows, cols = fine.shape
    count = rows // BLOCK
    n = lax.axis_index("cuts")
    lane = lane_index((count, LANES))
    per = LANES // BLOCK
    sources = [pick(n, [table.index(i) for i in range(slices)]) for table in partners(slices)]
    for k in range(cols // LANES // BLOCK):
        total = own[k]
        for source, x in zip(sources, received, strict=True):
            total = total + jnp.where(source < n, x[k], 0.0)
        for q in range(BLOCK):
            t = k * BLOCK + q
            up = jnp.take_along_axis(total, q * per + lane // BLOCK, axis=1)
            for i in range(BLOCK):
                tall[t, pl.ds(i, count, stride=BLOCK)] = up
            at = slice(t * LANES, (t + 1) * LANES)
            out[0, :, at] = fine[:, at] + tall[t]


def out_call(slices, fine, own, received):
    rows, cols = fine.shape
    return pl.pallas_call(
        functools.partial(out_kernel, slices),
        out_shape=jax.ShapeDtypeStruct((1, rows, cols), jnp.float32),
        in_specs=[VMEM] * (1 + slices),
        out_specs=VMEM,
        scratch_shapes=[pltpu.VMEM((cols // LANES, rows, LANES), jnp.float32)],
        compiler_params=COMPACT,
        name="total",
    )(fine, own, *received)


def iteration(states, stream):
    state = states[0]
    slices, bands = lax.axis_size("cuts"), lax.axis_size("space")
    rows = state.shape[0] // BLOCK
    up = [(i, (i + 1) % bands) for i in range(bands)]
    down = [(i, (i - 1) % bands) for i in range(bands)]
    twin = [(i, i ^ 1) for i in range(bands)]
    across = [(i, (i + 1 if i % 2 else i - 1) % bands) for i in range(bands)]

    def exchange(x, pairs):
        return lax.ppermute(x, "space", pairs)

    to_next, to_previous = rows_call(state, stream)
    low, high = exchange(to_next, up), exchange(to_previous, down)
    coarse = restrict_call(state, stream)
    paired = STAGES * (slices - 1) <= 2 * rows - SPILL and STAGES * slices <= 2 * rows
    if paired:
        pair = pair_call(coarse, exchange(coarse, twin))
        pair_near = exchange(pair, across)
        pair_far = exchange(pair_near, twin)
    tall = interleave_call(state, stream)
    fine, edge_twin, edge_across, spread = fine_call(*tall, low, high)
    if paired:
        whole, message = spread_call(spread, exchange(spread, twin), rows)
        near = exchange(message, across)
        far = exchange(near, twin)
        old, coefs = pair_prepare_call(slices, pair, pair_near, pair_far)
        *sent, own = pair_chain_call(slices, whole, near, far, old, coefs)
    else:
        *sent, own = wide_chain(slices, spread, coarse)
    from_twin, from_across = exchange(edge_twin, twin), exchange(edge_across, across)
    received = []
    for x, table in zip(sent, partners(slices), strict=True):
        received.append(lax.ppermute(x, "cuts", list(enumerate(table))))
    return out_call(slices, settle_call(fine, from_twin, from_across), own, received)


def solution(mesh):
    return jax.shard_map(
        iteration,
        mesh=mesh,
        in_specs=(P("cuts", "space", None), P("space", None)),
        out_specs=P("cuts", "space", None),
        check_vma=False,
    )
```

```python
import functools

import jax
import jax.numpy as jnp
from jax import lax
from jax.experimental import pallas as pl
from jax.experimental.pallas import tpu as pltpu
from jax.sharding import PartitionSpec as P

FINE_STEPS = 4
VISCOSITY = 0.2
FINE_DT = 0.25
BLOCK = 4
LANES = 128
SUB = 8
STAGES = 4
REACH = FINE_STEPS * STAGES // 2
SPILL = REACH // BLOCK
VMEM = pl.BlockSpec(memory_space=pltpu.VMEM)
CHUNK = 16
COMPACT = pltpu.CompilerParams(vmem_limit_bytes=12 * 2**20)


def lane_index(shape):
    return lax.broadcasted_iota(jnp.int32, shape, len(shape) - 1)


def horner(diffusion):
    c = 4.0 * diffusion
    b = 24.0**-0.25
    powers = (
        1 - c + c**2 / 2 - c**3 / 6 + c**4 / 24,
        1 - c + c**2 / 2 - c**3 / 6,
        (1 - c + c**2 / 2) / 2,
        (1 - c) / 6,
    )
    return b, [powers[k] / b**k for k in (3, 2, 1, 0)]


def neighbours(source, rows, group):
    tiles = source.shape[0]
    lo, hi = rows
    lane = lane_index((hi - lo, LANES))
    first, last = lane == 0, lane == LANES - 1
    groups = tiles // group

    def eastern(k):
        return pltpu.roll(source[k % groups * group, lo:hi], LANES - 1, 1)

    east_here, west_before = eastern(0), pltpu.roll(source[tiles - 1, lo:hi], 1, 1)
    for k in range(groups):
        east_after = eastern(k + 1)
        here = [source[k * group + i, lo:hi] for i in range(group)]
        west_here = pltpu.roll(here[-1], 1, 1)
        for i in range(group):
            east = here[i + 1] if i + 1 < group else jnp.where(last, east_after, east_here)
            west = here[i - 1] if i else jnp.where(first, west_before, west_here)
            yield k * group + i, east, west
        east_here, west_before = east_after, west_here


def set_coefs(psi, coefs, rows, scale, diffusion, group):
    lo, hi = rows
    b, _ = horner(diffusion)
    scale, diffusion = scale * b, diffusion * b
    for t, east, west in neighbours(psi, rows, group):
        u = scale * (psi[t, lo + 1 : hi + 1] - psi[t, lo - 1 : hi - 1])
        v = scale * (west - east)
        coefs[0, t, lo:hi] = diffusion - u
        coefs[1, t, lo:hi] = diffusion + u
        coefs[2, t, lo:hi] = diffusion - v
        coefs[3, t, lo:hi] = diffusion + v


def stage(source, a, out, coefs, rows, factor, group):
    chunk = CHUNK if group > 1 else rows[1] - rows[0]
    for lo in range(*rows, chunk):
        hi = min(lo + chunk, rows[1])
        for t, east, west in neighbours(source, (lo, hi), group):
            along = coefs[0, t, lo:hi] * east + coefs[1, t, lo:hi] * west
            across = coefs[2, t, lo:hi] * source[t, lo + 1 : hi + 1] + coefs[3, t, lo:hi] * source[t, lo - 1 : hi - 1]
            out[t, lo:hi] = (along + across) + factor * a[t, lo:hi]


def step(a, z, coefs, rows, diffusion, group):
    _, factors = horner(diffusion)
    for k in range(STAGES):
        source = a if k == 0 else z.at[(k - 1) % 2]
        stage(source, a, a if k == STAGES - 1 else z.at[k % 2], coefs, rows[k], factors[k], group)


def transposed(parts):
    lane = lane_index(parts[0].shape)
    for width in (LANES // 4, LANES // 2):
        keep = lane // width % 2 == 0
        apart = 4 * width // LANES
        out = list(parts)
        for i in range(4):
            if i & apart == 0:
                j = i + apart
                out[i] = jnp.where(keep, parts[i], pltpu.roll(parts[j], width, 1))
                out[j] = jnp.where(keep, pltpu.roll(parts[i], LANES - width, 1), parts[j])
        parts = out
    return parts


def interleaved(parts):
    lane = lane_index(parts[0].shape)
    at = lane % (LANES // BLOCK) * BLOCK + lane // (LANES // BLOCK)
    return transposed([jnp.take_along_axis(x, at, axis=1) for x in parts])


def in_order(parts):
    lane = lane_index(parts[0].shape)
    at = lane % BLOCK * (LANES // BLOCK) + lane // BLOCK
    return [jnp.take_along_axis(x, at, axis=1) for x in transposed(parts)]


def spread_tiles(take, tiles, put):
    for k in range(0, tiles, BLOCK):
        parts = [take(k + i) for i in range(BLOCK)]
        for i, x in enumerate(interleaved(parts)):
            put(k + i, x)


def pooled(take, tiles, put):
    for k in range(tiles // BLOCK):
        sums = [(take(t, 0) + take(t, 1)) + (take(t, 2) + take(t, 3)) for t in range(k * BLOCK, (k + 1) * BLOCK)]
        put(k, ((sums[0] + sums[1]) + (sums[2] + sums[3])) * (1.0 / (BLOCK * BLOCK)))


def rows_kernel(states, stream, to_twin, to_across, *here):
    here, sems = here[:2], here[2]
    last = states.shape[0] - REACH
    odd = band_of_pair()
    copies = [
        pltpu.make_async_copy(
            source.at[pl.ds(pl.multiple_of(first, SUB), REACH)], out.at[pl.ds(k * REACH, REACH)], sems.at[2 * j + k]
        )
        for j, (out, first) in enumerate(((to_twin, last * (1 - odd)), (to_across, last * odd)))
        for k, source in enumerate((states, stream))
    ]
    copies += [
        pltpu.make_async_copy(source, out, sems.at[4 + k])
        for k, (source, out) in enumerate(zip((states, stream), here, strict=True))
    ]
    for copy in copies:
        copy.start()
    for copy in copies:
        copy.wait()


def rows_call(states, stream):
    out = jax.ShapeDtypeStruct((2 * REACH, states.shape[1]), jnp.float32)
    own = jax.ShapeDtypeStruct(states.shape, jnp.float32)
    return pl.pallas_call(
        rows_kernel,
        out_shape=(out, out, own, own),
        in_specs=[pl.BlockSpec(memory_space=pltpu.HBM)] * 2,
        out_specs=(VMEM,) * 4,
        scratch_shapes=[pltpu.SemaphoreType.DMA((6,))],
        compiler_params=COMPACT,
        name="rows",
    )(*(pltpu.with_memory_space_constraint(x, pltpu.HBM) for x in (states, stream)))


def restrict_kernel(states, stream, out, tall):
    rows, cols = states.shape
    count = rows // BLOCK
    lane = lane_index((count, LANES))
    per = LANES // BLOCK
    for k, source in enumerate((states, stream)):
        for t in range(cols // LANES):
            tall[k, t] = source[:, t * LANES : (t + 1) * LANES]
        for c in range(cols // LANES // BLOCK):
            whole = jnp.zeros((count, LANES), jnp.float32)
            for q in range(BLOCK):
                part = [tall[k, c * BLOCK + q, pl.ds(i, count, stride=BLOCK)] for i in range(BLOCK)]
                x = (part[0] + part[1]) + (part[2] + part[3])
                x = x + pltpu.roll(x, LANES - 1, 1)
                x = x + pltpu.roll(x, LANES - 2, 1)
                x = jnp.take_along_axis(x, lane * BLOCK % LANES, axis=1)
                whole = jnp.where(lane // per == q, x, whole)
            out[c, k * count : (k + 1) * count] = whole * (1.0 / (BLOCK * BLOCK))


def restrict_call(states, stream):
    rows, cols = states.shape
    tiles = cols // LANES
    return pl.pallas_call(
        restrict_kernel,
        out_shape=jax.ShapeDtypeStruct((tiles // BLOCK, 2 * rows // BLOCK, LANES), jnp.float32),
        in_specs=[VMEM] * 2,
        out_specs=VMEM,
        scratch_shapes=[pltpu.VMEM((2, tiles, rows, LANES), jnp.float32)],
        compiler_params=COMPACT,
        name="restrict",
    )(states, stream)


def interleave_kernel(states, stream, *tall):
    for source, out in zip((states, stream), tall, strict=True):

        def keep(t, value, out=out):
            out[t] = value

        spread_tiles(lambda t, x=source: x[:, t * LANES : (t + 1) * LANES], source.shape[1] // LANES, keep)


def interleave_call(states, stream):
    rows, cols = states.shape
    tall = jax.ShapeDtypeStruct((cols // LANES, rows, LANES), jnp.float32)
    return pl.pallas_call(
        interleave_kernel,
        out_shape=(tall, tall),
        in_specs=[VMEM] * 2,
        out_specs=(VMEM,) * 2,
        compiler_params=COMPACT,
        name="interleave",
    )(states, stream)


def band_rows(rows):
    own = SUB + REACH
    spread = -(-(rows // BLOCK + 2 * SPILL) // SUB) * SUB
    return own, own + rows, SUB + max(BLOCK * spread, rows + 2 * REACH + SUB), spread


def inside_kernel(states, stream, levels, coefs, psi):
    tiles, rows, _ = states.shape
    own, top, size, _ = band_rows(rows)
    below, above = jnp.zeros((own, LANES), jnp.float32), jnp.zeros((size - top, LANES), jnp.float32)
    for t in range(tiles):
        levels[0, t, own:top] = states[t]
        psi[t, own:top] = stream[t]
        for buffer in (psi, levels.at[0], levels.at[REACH], levels.at[REACH + 1], levels.at[REACH + 2]):
            buffer[t, 0:own] = below
            buffer[t, top:size] = above
    diffusion = VISCOSITY * FINE_DT
    set_coefs(psi, coefs, (own, top), FINE_DT * 0.25, diffusion, BLOCK)
    _, factors = horner(diffusion)
    for n in range(REACH):
        base = levels.at[n // STAGES * STAGES]
        stage(levels.at[n], base, levels.at[n + 1], coefs, (own, top), factors[n % STAGES], BLOCK)


def inside_call(states, stream):
    tiles, rows, _ = states.shape
    size = band_rows(rows)[2]
    f32 = jnp.float32
    return pl.pallas_call(
        inside_kernel,
        out_shape=(
            jax.ShapeDtypeStruct((REACH + 3, tiles, size, LANES), f32),
            jax.ShapeDtypeStruct((4, tiles, size, LANES), f32),
            jax.ShapeDtypeStruct((tiles, size, LANES), f32),
        ),
        in_specs=[VMEM] * 2,
        out_specs=(VMEM,) * 3,
        compiler_params=COMPACT,
        name="inside",
    )(states, stream)


def fine_kernel(rows, twin, across, *refs):
    levels, coefs, psi, fine, edge_twin, edge_across, e_out = refs[3:]
    odd = band_of_pair() == 1
    tiles = psi.shape[0]
    own, top, _, spread = band_rows(rows)
    for k, buffer in enumerate((levels.at[0], psi)):

        def below(t, value, buffer=buffer):
            buffer[t, SUB:own] = value

        def above(t, value, buffer=buffer):
            buffer[t, top : top + REACH] = value

        def received(x, y, k=k):
            part = slice(k * REACH, (k + 1) * REACH)

            def take(t):
                at = slice(t * LANES, (t + 1) * LANES)
                return jnp.where(odd, x[part, at], y[part, at])

            return take

        spread_tiles(received(twin, across), tiles, below)
        spread_tiles(received(across, twin), tiles, above)
    diffusion = VISCOSITY * FINE_DT
    _, factors = horner(diffusion)
    for near in ((SUB, own + SUB), (top - SUB, top + REACH)):
        set_coefs(psi, coefs, near, FINE_DT * 0.25, diffusion, BLOCK)
    for n in range(REACH):
        base = levels.at[n // STAGES * STAGES]
        for near in ((SUB + n + 1, own + n + 1), (top - n - 1, top + REACH - n - 1)):
            stage(levels.at[n], base, levels.at[n + 1], coefs, near, factors[n % STAGES], BLOCK)
    a, z = levels.at[REACH], levels.at[REACH + 1 : REACH + 3]

    def rows_at(n):
        reach = min(n + -(rows + 2 * n) % SUB // 2, REACH)
        return (own - reach, top + reach)

    for n in range(0, REACH, STAGES):
        step(a, z, coefs, [rows_at(n + k) for k in range(1, STAGES + 1)], diffusion, BLOCK)
    for t in range(tiles):
        fine[t] = a[t, own:top]
        below, above = a[t, SUB:own], a[t, top : top + REACH]
        edge_twin[t] = jnp.where(odd, below, above)
        edge_across[t] = jnp.where(odd, above, below)

    def take(t, i):
        return a[t, pl.ds(SUB + i, spread, stride=BLOCK)]

    def put(k, value):
        e_out[k] = value

    pooled(take, tiles, put)


def fine_call(twin, across, levels, coefs, psi, rows):
    tiles = psi.shape[0]
    f32 = jnp.float32
    same = tuple(jax.ShapeDtypeStruct(x.shape, f32) for x in (levels, coefs, psi))
    return pl.pallas_call(
        functools.partial(fine_kernel, rows),
        out_shape=same
        + (
            jax.ShapeDtypeStruct((tiles, rows, LANES), f32),
            jax.ShapeDtypeStruct((tiles, REACH, LANES), f32),
            jax.ShapeDtypeStruct((tiles, REACH, LANES), f32),
            jax.ShapeDtypeStruct((tiles // BLOCK, band_rows(rows)[3], LANES), f32),
        ),
        in_specs=[VMEM] * 5,
        out_specs=(VMEM,) * 7,
        input_output_aliases={2: 0, 3: 1, 4: 2},
        compiler_params=COMPACT,
        name="fine",
    )(twin, across, levels, coefs, psi)[3:]


def pair_kernel(mine, theirs, out):
    tiles, both, _ = mine.shape
    rows = both // 2
    odd = lax.rem(lax.axis_index("space"), 2) == 1
    for t in range(tiles):
        lower = jnp.where(odd, theirs[t], mine[t])
        upper = jnp.where(odd, mine[t], theirs[t])
        for k in range(2):
            out[t, 2 * k * rows : (2 * k + 1) * rows] = lower[k * rows : (k + 1) * rows]
            out[t, (2 * k + 1) * rows : (2 * k + 2) * rows] = upper[k * rows : (k + 1) * rows]


def pair_call(mine, theirs):
    tiles, both, _ = mine.shape
    return pl.pallas_call(
        pair_kernel,
        out_shape=jax.ShapeDtypeStruct((tiles, 2 * both, LANES), jnp.float32),
        in_specs=[VMEM] * 2,
        out_specs=VMEM,
        compiler_params=COMPACT,
        name="pair",
    )(mine, theirs)


def spread_kernel(rows, mine, theirs, whole, message):
    tiles, spread, _ = mine.shape
    odd = lax.rem(lax.axis_index("space"), 2) == 1
    for t in range(tiles):
        lower = jnp.where(odd, theirs[t], mine[t])
        upper = jnp.where(odd, mine[t], theirs[t])
        whole[t, 0:spread] = lower
        whole[t, spread:] = jnp.zeros((whole.shape[1] - spread, LANES), jnp.float32)
        whole[t, rows : rows + spread] = whole[t, rows : rows + spread] + upper
        message[t] = jnp.where(odd, whole[t, 2 * SPILL : 2 * SPILL + 2 * rows], whole[t, 0 : 2 * rows])


def spread_call(mine, theirs, rows):
    tiles, spread, _ = mine.shape
    f32 = jnp.float32
    return pl.pallas_call(
        functools.partial(spread_kernel, rows),
        out_shape=(
            jax.ShapeDtypeStruct((tiles, rows + spread, LANES), f32),
            jax.ShapeDtypeStruct((tiles, 2 * rows, LANES), f32),
        ),
        in_specs=[VMEM] * 2,
        out_specs=(VMEM,) * 2,
        compiler_params=COMPACT,
        name="spread",
    )(mine, theirs)


def partners(slices):
    if slices == 4:
        return [(2, 3, 1, 0), (3, 2, 0, 1), (1, 0, 3, 2)]
    return [tuple((i + k) % slices for i in range(slices)) for k in range(1, slices)]


def pick(n, table):
    return sum(jnp.where(n == i, x, 0) for i, x in enumerate(table))


def coarse_rows(reach, rows, pads):
    reach = min(reach + -(rows + 2 * reach) % SUB // 2, pads)
    return (SUB + pads - reach, SUB + pads + rows + reach)


def coarse_diffusion():
    return VISCOSITY * FINE_DT * FINE_STEPS / (BLOCK * BLOCK)


def prepare(psi, old, z, coefs, rows, pads, slices):
    step_size, spacing = FINE_DT * FINE_STEPS, float(BLOCK)
    diffusion = coarse_diffusion()
    set_coefs(psi, coefs, (SUB, SUB + rows + 2 * pads), step_size / (4.0 * spacing * spacing), diffusion, 1)
    reach = STAGES * slices
    step(old, z, coefs, [coarse_rows(reach - k, rows, pads) for k in range(1, STAGES + 1)], diffusion, 1)


def clear_edges(buffers):
    edge = jnp.zeros((SUB, LANES), jnp.float32)
    for buffer in buffers:
        for t in range(buffer.shape[0]):
            buffer[t, 0:SUB] = edge
            buffer[t, buffer.shape[1] - SUB :] = edge


def band_of_pair():
    return lax.rem(lax.axis_index("space"), 2)


def pair_prepare_kernel(slices, rows, pair, near, far, old, coefs, psi, z, wide):
    odd = band_of_pair() == 1
    pads = 2 * rows
    first = pl.multiple_of(rows * band_of_pair(), SUB)
    clear_edges((old, psi, z.at[0], z.at[1]))
    for k, out in enumerate((old, psi)):
        part = slice(2 * k * rows, 2 * (k + 1) * rows)
        for t in range(out.shape[0]):
            wide[t, 0:pads] = jnp.where(odd, far[t, part], near[t, part])
            wide[t, pads : 2 * pads] = pair[t, part]
            wide[t, 2 * pads : 3 * pads] = jnp.where(odd, near[t, part], far[t, part])
            out[t, SUB : SUB + rows + 2 * pads] = wide[t, pl.ds(first, rows + 2 * pads)]
    prepare(psi, old, z, coefs, rows, pads, slices)


def prepare_shapes(tiles, size):
    f32 = jnp.float32
    return (
        (jax.ShapeDtypeStruct((tiles, size, LANES), f32), jax.ShapeDtypeStruct((4, tiles, size, LANES), f32)),
        [pltpu.VMEM((tiles, size, LANES), f32), pltpu.VMEM((2, tiles, size, LANES), f32)],
    )


def pair_prepare_call(slices, pair, near, far):
    tiles, total, _ = pair.shape
    rows = total // 4
    shapes, scratch = prepare_shapes(tiles, 5 * rows + 2 * SUB)
    return pl.pallas_call(
        functools.partial(pair_prepare_kernel, slices, rows),
        out_shape=shapes,
        in_specs=[VMEM] * 3,
        out_specs=(VMEM,) * 2,
        scratch_shapes=scratch + [pltpu.VMEM((tiles, 6 * rows, LANES), jnp.float32)],
        compiler_params=COMPACT,
        name="prepare",
    )(pair, near, far)


def chain(gap, old, z, coefs, powers, outs, rows, pads):
    slices = len(outs)
    n = lax.axis_index("cuts")
    own = slice(SUB + pads, SUB + pads + rows)
    extent = slice(*coarse_rows(STAGES * (slices - 1), rows, pads))
    for t in range(gap.shape[0]):
        start = jnp.where(n == 0, old[t, extent], 0.0)
        gap[t, extent] = (gap[t, extent] - old[t, extent]) + start
        mine = old[t, own]
        outs[-1][t] = jnp.where(n == 0, mine, 0.0) - mine
    reach = STAGES * (slices - 1)
    for j in range(1, slices):
        step(gap, z, coefs, [coarse_rows(reach - k, rows, pads) for k in range(1, STAGES + 1)], coarse_diffusion(), 1)
        reach -= STAGES
        for t in range(gap.shape[0]):
            powers[j, t] = gap[t, own]
    for out, table in zip(outs[:-1], partners(slices), strict=True):
        ahead = pick(n, [max(x - i, 1) for i, x in enumerate(table)])
        for t in range(gap.shape[0]):
            out[t] = powers[ahead, t]


def pair_chain_kernel(slices, rows, whole, message, passed, old, coefs, *refs):
    outs, (gap, z, powers, wide) = refs[:slices], refs[slices:]
    odd = band_of_pair() == 1
    pads = 2 * rows
    first = pl.multiple_of(rows * band_of_pair(), SUB)
    clear_edges((gap, z.at[0], z.at[1]))
    for t in range(gap.shape[0]):
        wide[t] = jnp.zeros(wide.shape[1:], jnp.float32)
        at = pads - SPILL
        wide[t, at : at + whole.shape[1]] = whole[t]
        for at, x in (
            (pads + SPILL - 2 * rows, jnp.where(odd, passed[t], message[t])),
            (pads - SPILL + 2 * rows, jnp.where(odd, message[t], passed[t])),
        ):
            wide[t, at : at + 2 * rows] = wide[t, at : at + 2 * rows] + x
        gap[t, SUB : SUB + rows + 2 * pads] = wide[t, pl.ds(first, rows + 2 * pads)]
    chain(gap, old, z, coefs, powers, outs, rows, pads)


def chain_shapes(tiles, size, slices, rows):
    f32 = jnp.float32
    return (
        (jax.ShapeDtypeStruct((tiles, rows, LANES), f32),) * slices,
        [
            pltpu.VMEM((tiles, size, LANES), f32),
            pltpu.VMEM((2, tiles, size, LANES), f32),
            pltpu.VMEM((slices, tiles, rows, LANES), f32),
        ],
    )


def pair_chain_call(slices, whole, message, passed, old, coefs):
    tiles = whole.shape[0]
    rows = message.shape[1] // 2
    shapes, scratch = chain_shapes(tiles, old.shape[1], slices, rows)
    return pl.pallas_call(
        functools.partial(pair_chain_kernel, slices, rows),
        out_shape=shapes,
        in_specs=[VMEM] * 5,
        out_specs=(VMEM,) * slices,
        scratch_shapes=scratch + [pltpu.VMEM((tiles, 6 * rows, LANES), jnp.float32)],
        compiler_params=COMPACT,
        name="coarse",
    )(whole, message, passed, old, coefs)


def wide_chain_kernel(slices, rows, pads, gap_in, old_in, psi_in, *refs):
    outs, (gap, z, powers, old, coefs, psi) = refs[:slices], refs[slices:]
    clear_edges((gap, old, psi, z.at[0], z.at[1]))
    for source, out in ((gap_in, gap), (old_in, old), (psi_in, psi)):
        for t in range(gap.shape[0]):
            out[t, SUB : SUB + rows + 2 * pads] = source[t]
    prepare(psi, old, z, coefs, rows, pads, slices)
    chain(gap, old, z, coefs, powers, outs, rows, pads)


def wide_chain(slices, spread, coarse):
    tiles, both, _ = coarse.shape
    rows = both // 2
    bands = lax.axis_size("space")
    total = bands * rows
    length = spread.shape[1]
    every = lax.all_gather(spread, "space")
    gap = jnp.zeros((tiles, total, LANES), jnp.float32)
    for b in range(bands):
        at = (b * rows - SPILL + jnp.arange(length)) % total
        gap = gap.at[:, at].add(every[b])
    every = lax.all_gather(coarse, "space")
    old, psi = (jnp.moveaxis(every[:, :, k * rows : (k + 1) * rows], 0, 1).reshape(tiles, total, LANES) for k in range(2))
    pads = -(-STAGES * slices // SUB) * SUB
    at = (lax.axis_index("space") * rows - pads + jnp.arange(rows + 2 * pads)) % total
    size = rows + 2 * pads + 2 * SUB
    shapes, scratch = chain_shapes(tiles, size, slices, rows)
    more = [pltpu.VMEM(x.shape, x.dtype) for x in prepare_shapes(tiles, size)[0]]
    return pl.pallas_call(
        functools.partial(wide_chain_kernel, slices, rows, pads),
        out_shape=shapes,
        in_specs=[VMEM] * 3,
        out_specs=(VMEM,) * slices,
        scratch_shapes=scratch + more + [pltpu.VMEM((tiles, size, LANES), jnp.float32)],
        compiler_params=COMPACT,
        name="coarse",
    )(*(jnp.take(x, at, axis=1) for x in (gap, old, psi)))


def settle_kernel(fine, from_twin, from_across, out, tall):
    tiles, rows, _ = fine.shape
    odd = band_of_pair() == 1
    for t in range(tiles):
        tall[t, 0:REACH] = fine[t, 0:REACH] + jnp.where(odd, from_twin[t], from_across[t])
        tall[t, REACH : rows - REACH] = fine[t, REACH : rows - REACH]
        tall[t, rows - REACH : rows] = fine[t, rows - REACH : rows] + jnp.where(odd, from_across[t], from_twin[t])
    for k in range(0, tiles, BLOCK):
        for i, x in enumerate(in_order([tall[k + i] for i in range(BLOCK)])):
            out[:, (k + i) * LANES : (k + i + 1) * LANES] = x


def settle_call(fine, from_twin, from_across):
    tiles, rows, _ = fine.shape
    return pl.pallas_call(
        settle_kernel,
        out_shape=jax.ShapeDtypeStruct((rows, tiles * LANES), jnp.float32),
        in_specs=[VMEM] * 3,
        out_specs=VMEM,
        scratch_shapes=[pltpu.VMEM((tiles, rows, LANES), jnp.float32)],
        compiler_params=COMPACT,
        name="settle",
    )(fine, from_twin, from_across)


def out_kernel(slices, fine, own, *refs):
    received, (out, tall) = refs[: slices - 1], refs[slices - 1 :]
    rows, cols = fine.shape
    count = rows // BLOCK
    n = lax.axis_index("cuts")
    lane = lane_index((count, LANES))
    per = LANES // BLOCK
    sources = [pick(n, [table.index(i) for i in range(slices)]) for table in partners(slices)]
    for k in range(cols // LANES // BLOCK):
        total = own[k]
        for source, x in zip(sources, received, strict=True):
            total = total + jnp.where(source < n, x[k], 0.0)
        for q in range(BLOCK):
            t = k * BLOCK + q
            up = jnp.take_along_axis(total, q * per + lane // BLOCK, axis=1)
            for i in range(BLOCK):
                tall[t, pl.ds(i, count, stride=BLOCK)] = up
            at = slice(t * LANES, (t + 1) * LANES)
            out[0, :, at] = fine[:, at] + tall[t]


def out_call(slices, fine, own, received):
    rows, cols = fine.shape
    return pl.pallas_call(
        functools.partial(out_kernel, slices),
        out_shape=jax.ShapeDtypeStruct((1, rows, cols), jnp.float32),
        in_specs=[VMEM] * (1 + slices),
        out_specs=VMEM,
        scratch_shapes=[pltpu.VMEM((cols // LANES, rows, LANES), jnp.float32)],
        compiler_params=COMPACT,
        name="total",
    )(fine, own, *received)


def iteration(states, stream):
    state = states[0]
    slices, bands = lax.axis_size("cuts"), lax.axis_size("space")
    rows = state.shape[0] // BLOCK
    twin = [(i, i ^ 1) for i in range(bands)]
    across = [(i, (i + 1 if i % 2 else i - 1) % bands) for i in range(bands)]

    def exchange(x, pairs):
        return lax.ppermute(x, "space", pairs)

    to_twin, to_across, state, stream = rows_call(state, stream)
    rows_across, rows_twin = exchange(to_across, across), exchange(to_twin, twin)
    coarse = restrict_call(state, stream)
    paired = STAGES * (slices - 1) <= 2 * rows - SPILL and STAGES * slices <= 2 * rows
    if paired:
        pair = pair_call(coarse, exchange(coarse, twin))
        pair_near = exchange(pair, across)
        pair_far = exchange(pair_near, twin)
    tall = interleave_call(state, stream)
    begun = inside_call(*tall)
    fine, edge_twin, edge_across, spread = fine_call(rows_twin, rows_across, *begun, state.shape[0])
    if paired:
        whole, message = spread_call(spread, exchange(spread, twin), rows)
        near = exchange(message, across)
        far = exchange(near, twin)
        old, coefs = pair_prepare_call(slices, pair, pair_near, pair_far)
        *sent, own = pair_chain_call(slices, whole, near, far, old, coefs)
    else:
        *sent, own = wide_chain(slices, spread, coarse)
    from_twin, from_across = exchange(edge_twin, twin), exchange(edge_across, across)
    received = []
    for x, table in zip(sent, partners(slices), strict=True):
        received.append(lax.ppermute(x, "cuts", list(enumerate(table))))
    return out_call(slices, settle_call(fine, from_twin, from_across), own, received)


def solution(mesh):
    return jax.shard_map(
        iteration,
        mesh=mesh,
        in_specs=(P("cuts", "space", None), P("space", None)),
        out_specs=P("cuts", "space", None),
        check_vma=False,
    )
```

```python
import functools

import jax
import jax.numpy as jnp
from jax import lax
from jax.experimental import pallas as pl
from jax.experimental.pallas import tpu as pltpu
from jax.sharding import PartitionSpec as P

FINE_STEPS = 4
VISCOSITY = 0.2
FINE_DT = 0.25
BLOCK = 4
LANES = 128
SUB = 8
STAGES = 4
REACH = FINE_STEPS * STAGES // 2
SPILL = REACH // BLOCK
VMEM = pl.BlockSpec(memory_space=pltpu.VMEM)
CHUNK = 16
COMPACT = pltpu.CompilerParams(vmem_limit_bytes=12 * 2**20)


def lane_index(shape):
    return lax.broadcasted_iota(jnp.int32, shape, len(shape) - 1)


def horner(diffusion):
    c = 4.0 * diffusion
    b = 24.0**-0.25
    powers = (
        1 - c + c**2 / 2 - c**3 / 6 + c**4 / 24,
        1 - c + c**2 / 2 - c**3 / 6,
        (1 - c + c**2 / 2) / 2,
        (1 - c) / 6,
    )
    return b, [powers[k] / b**k for k in (3, 2, 1, 0)]


def neighbours(source, rows, group, begin):
    tiles = source.shape[0]
    lo, hi = rows
    lane = lane_index((hi - lo, LANES))
    first, last = lane == 0, lane == LANES - 1
    groups = tiles // group

    def eastern(k):
        return pltpu.roll(source[k % groups * group, lo:hi], LANES - 1, 1)

    def western(k):
        return pltpu.roll(source[k % groups * group + group - 1, lo:hi], 1, 1)

    east_here, west_before = eastern(begin), western(begin - 1)
    for k in range(begin, begin + groups):
        k_tile = k % groups * group
        east_after = eastern(k + 1)
        here = [source[k_tile + i, lo:hi] for i in range(group)]
        west_here = pltpu.roll(here[-1], 1, 1)
        for i in range(group):
            east = here[i + 1] if i + 1 < group else jnp.where(last, east_after, east_here)
            west = here[i - 1] if i else jnp.where(first, west_before, west_here)
            yield k_tile + i, east, west
        east_here, west_before = east_after, west_here


def set_coefs(psi, coefs, rows, scale, diffusion, group):
    lo, hi = rows
    b, _ = horner(diffusion)
    scale, diffusion = scale * b, diffusion * b
    for t, east, west in neighbours(psi, rows, group, 0):
        u = scale * (psi[t, lo + 1 : hi + 1] - psi[t, lo - 1 : hi - 1])
        v = scale * (west - east)
        coefs[0, t, lo:hi] = diffusion - u
        coefs[1, t, lo:hi] = diffusion + u
        coefs[2, t, lo:hi] = diffusion - v
        coefs[3, t, lo:hi] = diffusion + v


def stage(source, a, out, coefs, rows, factor, group, begin):
    chunk = CHUNK if group > 1 else rows[1] - rows[0]
    for lo in range(*rows, chunk):
        hi = min(lo + chunk, rows[1])
        for t, east, west in neighbours(source, (lo, hi), group, begin):
            along = coefs[0, t, lo:hi] * east + coefs[1, t, lo:hi] * west
            across = coefs[2, t, lo:hi] * source[t, lo + 1 : hi + 1] + coefs[3, t, lo:hi] * source[t, lo - 1 : hi - 1]
            out[t, lo:hi] = (along + across) + factor * a[t, lo:hi]


def step(a, z, coefs, rows, diffusion, group):
    _, factors = horner(diffusion)
    for k in range(STAGES):
        source = a if k == 0 else z.at[(k - 1) % 2]
        stage(source, a, a if k == STAGES - 1 else z.at[k % 2], coefs, rows[k], factors[k], group, k)


def transposed(parts):
    lane = lane_index(parts[0].shape)
    for width in (LANES // 4, LANES // 2):
        keep = lane // width % 2 == 0
        apart = 4 * width // LANES
        out = list(parts)
        for i in range(4):
            if i & apart == 0:
                j = i + apart
                out[i] = jnp.where(keep, parts[i], pltpu.roll(parts[j], width, 1))
                out[j] = jnp.where(keep, pltpu.roll(parts[i], LANES - width, 1), parts[j])
        parts = out
    return parts


def interleaved(parts):
    lane = lane_index(parts[0].shape)
    at = lane % (LANES // BLOCK) * BLOCK + lane // (LANES // BLOCK)
    return transposed([jnp.take_along_axis(x, at, axis=1) for x in parts])


def in_order(parts):
    lane = lane_index(parts[0].shape)
    at = lane % BLOCK * (LANES // BLOCK) + lane // BLOCK
    return [jnp.take_along_axis(x, at, axis=1) for x in transposed(parts)]


def spread_tiles(take, tiles, put):
    for k in range(0, tiles, BLOCK):
        parts = [take(k + i) for i in range(BLOCK)]
        for i, x in enumerate(interleaved(parts)):
            put(k + i, x)


def pooled(take, tiles, put):
    for k in range(tiles // BLOCK):
        sums = [(take(t, 0) + take(t, 1)) + (take(t, 2) + take(t, 3)) for t in range(k * BLOCK, (k + 1) * BLOCK)]
        put(k, ((sums[0] + sums[1]) + (sums[2] + sums[3])) * (1.0 / (BLOCK * BLOCK)))


def rows_kernel(states, stream, to_twin, to_across, *here):
    here, sems = here[:2], here[2]
    last = states.shape[0] - REACH
    odd = band_of_pair()
    copies = [
        pltpu.make_async_copy(
            source.at[pl.ds(pl.multiple_of(first, SUB), REACH)], out.at[pl.ds(k * REACH, REACH)], sems.at[2 * j + k]
        )
        for j, (out, first) in enumerate(((to_twin, last * (1 - odd)), (to_across, last * odd)))
        for k, source in enumerate((states, stream))
    ]
    copies += [
        pltpu.make_async_copy(source, out, sems.at[4 + k])
        for k, (source, out) in enumerate(zip((states, stream), here, strict=True))
    ]
    for copy in copies:
        copy.start()
    for copy in copies:
        copy.wait()


def rows_call(states, stream):
    out = jax.ShapeDtypeStruct((2 * REACH, states.shape[1]), jnp.float32)
    own = jax.ShapeDtypeStruct(states.shape, jnp.float32)
    return pl.pallas_call(
        rows_kernel,
        out_shape=(out, out, own, own),
        in_specs=[pl.BlockSpec(memory_space=pltpu.HBM)] * 2,
        out_specs=(VMEM,) * 4,
        scratch_shapes=[pltpu.SemaphoreType.DMA((6,))],
        compiler_params=COMPACT,
        name="rows",
    )(*(pltpu.with_memory_space_constraint(x, pltpu.HBM) for x in (states, stream)))


def restrict_kernel(states, stream, out, tall):
    rows, cols = states.shape
    count = rows // BLOCK
    lane = lane_index((count, LANES))
    per = LANES // BLOCK
    for k, source in enumerate((states, stream)):
        for t in range(cols // LANES):
            tall[k, t] = source[:, t * LANES : (t + 1) * LANES]
        for c in range(cols // LANES // BLOCK):
            whole = jnp.zeros((count, LANES), jnp.float32)
            for q in range(BLOCK):
                part = [tall[k, c * BLOCK + q, pl.ds(i, count, stride=BLOCK)] for i in range(BLOCK)]
                x = (part[0] + part[1]) + (part[2] + part[3])
                x = x + pltpu.roll(x, LANES - 1, 1)
                x = x + pltpu.roll(x, LANES - 2, 1)
                x = jnp.take_along_axis(x, lane * BLOCK % LANES, axis=1)
                whole = jnp.where(lane // per == q, x, whole)
            out[c, k * count : (k + 1) * count] = whole * (1.0 / (BLOCK * BLOCK))


def restrict_call(states, stream):
    rows, cols = states.shape
    tiles = cols // LANES
    return pl.pallas_call(
        restrict_kernel,
        out_shape=jax.ShapeDtypeStruct((tiles // BLOCK, 2 * rows // BLOCK, LANES), jnp.float32),
        in_specs=[VMEM] * 2,
        out_specs=VMEM,
        scratch_shapes=[pltpu.VMEM((2, tiles, rows, LANES), jnp.float32)],
        compiler_params=COMPACT,
        name="restrict",
    )(states, stream)


def interleave_kernel(states, stream, *tall):
    for source, out in zip((states, stream), tall, strict=True):

        def keep(t, value, out=out):
            out[t] = value

        spread_tiles(lambda t, x=source: x[:, t * LANES : (t + 1) * LANES], source.shape[1] // LANES, keep)


def interleave_call(states, stream):
    rows, cols = states.shape
    tall = jax.ShapeDtypeStruct((cols // LANES, rows, LANES), jnp.float32)
    return pl.pallas_call(
        interleave_kernel,
        out_shape=(tall, tall),
        in_specs=[VMEM] * 2,
        out_specs=(VMEM,) * 2,
        compiler_params=COMPACT,
        name="interleave",
    )(states, stream)


def band_rows(rows):
    own = SUB + REACH
    spread = -(-(rows // BLOCK + 2 * SPILL) // SUB) * SUB
    return own, own + rows, SUB + max(BLOCK * spread, rows + 2 * REACH + SUB), spread


def side(rows, low, received, levels, coefs, psi):
    own, top, _, _ = band_rows(rows)
    tiles = psi.shape[0]
    first = SUB if low else top
    for k, buffer in enumerate((levels.at[0], psi)):

        def take(t, k=k):
            return received[k * REACH : (k + 1) * REACH, t * LANES : (t + 1) * LANES]

        def put(t, value, buffer=buffer):
            buffer[t, first : first + REACH] = value

        spread_tiles(take, tiles, put)
    diffusion = VISCOSITY * FINE_DT
    _, factors = horner(diffusion)
    set_coefs(psi, coefs, (SUB, own + SUB) if low else (top - SUB, top + REACH), FINE_DT * 0.25, diffusion, BLOCK)
    for n in range(REACH):
        base = levels.at[n // STAGES * STAGES]
        at = SUB + n + 1 if low else top - n - 1
        stage(levels.at[n], base, levels.at[n + 1], coefs, (at, at + REACH), factors[n % STAGES], BLOCK, n)


def either_side(low, rows, received, levels, coefs, psi):
    for flag in (True, False):

        @pl.when(low == flag)
        def _(flag=flag):
            side(rows, flag, received, levels, coefs, psi)


def inside_kernel(states, stream, twin, levels, coefs, psi):
    tiles, rows, _ = states.shape
    own, top, size, _ = band_rows(rows)
    below, above = jnp.zeros((own, LANES), jnp.float32), jnp.zeros((size - top, LANES), jnp.float32)
    for t in range(tiles):
        levels[0, t, own:top] = states[t]
        psi[t, own:top] = stream[t]
        for buffer in (psi, levels.at[0], levels.at[REACH], levels.at[REACH + 1], levels.at[REACH + 2]):
            buffer[t, 0:own] = below
            buffer[t, top:size] = above
    diffusion = VISCOSITY * FINE_DT
    set_coefs(psi, coefs, (own, top), FINE_DT * 0.25, diffusion, BLOCK)
    _, factors = horner(diffusion)
    for n in range(REACH):
        base = levels.at[n // STAGES * STAGES]
        wider = -(rows - 2 * (n + 1)) % SUB // 2
        at = (own + n + 1 - wider, top - n - 1 + wider)
        stage(levels.at[n], base, levels.at[n + 1], coefs, at, factors[n % STAGES], BLOCK, n)
    either_side(band_of_pair() == 1, rows, twin, levels, coefs, psi)


def inside_call(states, stream, twin):
    tiles, rows, _ = states.shape
    size = band_rows(rows)[2]
    f32 = jnp.float32
    return pl.pallas_call(
        inside_kernel,
        out_shape=(
            jax.ShapeDtypeStruct((REACH + 3, tiles, size, LANES), f32),
            jax.ShapeDtypeStruct((4, tiles, size, LANES), f32),
            jax.ShapeDtypeStruct((tiles, size, LANES), f32),
        ),
        in_specs=[VMEM] * 3,
        out_specs=(VMEM,) * 3,
        compiler_params=COMPACT,
        name="inside",
    )(states, stream, twin)


def fine_kernel(rows, across, *refs):
    levels, coefs, psi, fine, edge_twin, edge_across, e_out = refs[3:]
    odd = band_of_pair() == 1
    tiles = psi.shape[0]
    own, top, _, spread = band_rows(rows)
    diffusion = VISCOSITY * FINE_DT
    either_side(band_of_pair() == 0, rows, across, levels, coefs, psi)
    a, z = levels.at[REACH], levels.at[REACH + 1 : REACH + 3]

    def rows_at(n):
        reach = min(n + -(rows + 2 * n) % SUB // 2, REACH)
        return (own - reach, top + reach)

    for n in range(0, REACH, STAGES):
        step(a, z, coefs, [rows_at(n + k) for k in range(1, STAGES + 1)], diffusion, BLOCK)
    for t in range(tiles):
        fine[t] = a[t, own:top]
        below, above = a[t, SUB:own], a[t, top : top + REACH]
        edge_twin[t] = jnp.where(odd, below, above)
        edge_across[t] = jnp.where(odd, above, below)

    def take(t, i):
        return a[t, pl.ds(SUB + i, spread, stride=BLOCK)]

    def put(k, value):
        e_out[k] = value

    pooled(take, tiles, put)


def fine_call(across, levels, coefs, psi, rows):
    tiles = psi.shape[0]
    f32 = jnp.float32
    same = tuple(jax.ShapeDtypeStruct(x.shape, f32) for x in (levels, coefs, psi))
    return pl.pallas_call(
        functools.partial(fine_kernel, rows),
        out_shape=same
        + (
            jax.ShapeDtypeStruct((tiles, rows, LANES), f32),
            jax.ShapeDtypeStruct((tiles, REACH, LANES), f32),
            jax.ShapeDtypeStruct((tiles, REACH, LANES), f32),
            jax.ShapeDtypeStruct((tiles // BLOCK, band_rows(rows)[3], LANES), f32),
        ),
        in_specs=[VMEM] * 4,
        out_specs=(VMEM,) * 7,
        input_output_aliases={1: 0, 2: 1, 3: 2},
        compiler_params=COMPACT,
        name="fine",
    )(across, levels, coefs, psi)[3:]


def pair_kernel(mine, theirs, out):
    tiles, both, _ = mine.shape
    rows = both // 2
    odd = lax.rem(lax.axis_index("space"), 2) == 1
    for t in range(tiles):
        lower = jnp.where(odd, theirs[t], mine[t])
        upper = jnp.where(odd, mine[t], theirs[t])
        for k in range(2):
            out[t, 2 * k * rows : (2 * k + 1) * rows] = lower[k * rows : (k + 1) * rows]
            out[t, (2 * k + 1) * rows : (2 * k + 2) * rows] = upper[k * rows : (k + 1) * rows]


def pair_call(mine, theirs):
    tiles, both, _ = mine.shape
    return pl.pallas_call(
        pair_kernel,
        out_shape=jax.ShapeDtypeStruct((tiles, 2 * both, LANES), jnp.float32),
        in_specs=[VMEM] * 2,
        out_specs=VMEM,
        compiler_params=COMPACT,
        name="pair",
    )(mine, theirs)


def spread_kernel(rows, mine, theirs, whole, message):
    tiles, spread, _ = mine.shape
    odd = lax.rem(lax.axis_index("space"), 2) == 1
    for t in range(tiles):
        lower = jnp.where(odd, theirs[t], mine[t])
        upper = jnp.where(odd, mine[t], theirs[t])
        whole[t, 0:spread] = lower
        whole[t, spread:] = jnp.zeros((whole.shape[1] - spread, LANES), jnp.float32)
        whole[t, rows : rows + spread] = whole[t, rows : rows + spread] + upper
        message[t] = jnp.where(odd, whole[t, 2 * SPILL : 2 * SPILL + 2 * rows], whole[t, 0 : 2 * rows])


def spread_call(mine, theirs, rows):
    tiles, spread, _ = mine.shape
    f32 = jnp.float32
    return pl.pallas_call(
        functools.partial(spread_kernel, rows),
        out_shape=(
            jax.ShapeDtypeStruct((tiles, rows + spread, LANES), f32),
            jax.ShapeDtypeStruct((tiles, 2 * rows, LANES), f32),
        ),
        in_specs=[VMEM] * 2,
        out_specs=(VMEM,) * 2,
        compiler_params=COMPACT,
        name="spread",
    )(mine, theirs)


def partners(slices):
    if slices == 4:
        return [(2, 3, 1, 0), (3, 2, 0, 1), (1, 0, 3, 2)]
    return [tuple((i + k) % slices for i in range(slices)) for k in range(1, slices)]


def pick(n, table):
    return sum(jnp.where(n == i, x, 0) for i, x in enumerate(table))


def coarse_rows(reach, rows, pads):
    reach = min(reach + -(rows + 2 * reach) % SUB // 2, pads)
    return (SUB + pads - reach, SUB + pads + rows + reach)


def coarse_diffusion():
    return VISCOSITY * FINE_DT * FINE_STEPS / (BLOCK * BLOCK)


def prepare(psi, old, z, coefs, rows, pads, slices):
    step_size, spacing = FINE_DT * FINE_STEPS, float(BLOCK)
    diffusion = coarse_diffusion()
    set_coefs(psi, coefs, (SUB, SUB + rows + 2 * pads), step_size / (4.0 * spacing * spacing), diffusion, 1)
    reach = STAGES * slices
    step(old, z, coefs, [coarse_rows(reach - k, rows, pads) for k in range(1, STAGES + 1)], diffusion, 1)


def clear_edges(buffers):
    edge = jnp.zeros((SUB, LANES), jnp.float32)
    for buffer in buffers:
        for t in range(buffer.shape[0]):
            buffer[t, 0:SUB] = edge
            buffer[t, buffer.shape[1] - SUB :] = edge


def band_of_pair():
    return lax.rem(lax.axis_index("space"), 2)


def pair_prepare_kernel(slices, rows, pair, near, far, old, coefs, psi, z, wide):
    odd = band_of_pair() == 1
    pads = 2 * rows
    first = pl.multiple_of(rows * band_of_pair(), SUB)
    clear_edges((old, psi, z.at[0], z.at[1]))
    for k, out in enumerate((old, psi)):
        part = slice(2 * k * rows, 2 * (k + 1) * rows)
        for t in range(out.shape[0]):
            wide[t, 0:pads] = jnp.where(odd, far[t, part], near[t, part])
            wide[t, pads : 2 * pads] = pair[t, part]
            wide[t, 2 * pads : 3 * pads] = jnp.where(odd, near[t, part], far[t, part])
            out[t, SUB : SUB + rows + 2 * pads] = wide[t, pl.ds(first, rows + 2 * pads)]
    prepare(psi, old, z, coefs, rows, pads, slices)


def prepare_shapes(tiles, size):
    f32 = jnp.float32
    return (
        (jax.ShapeDtypeStruct((tiles, size, LANES), f32), jax.ShapeDtypeStruct((4, tiles, size, LANES), f32)),
        [pltpu.VMEM((tiles, size, LANES), f32), pltpu.VMEM((2, tiles, size, LANES), f32)],
    )


def pair_prepare_call(slices, pair, near, far):
    tiles, total, _ = pair.shape
    rows = total // 4
    shapes, scratch = prepare_shapes(tiles, 5 * rows + 2 * SUB)
    return pl.pallas_call(
        functools.partial(pair_prepare_kernel, slices, rows),
        out_shape=shapes,
        in_specs=[VMEM] * 3,
        out_specs=(VMEM,) * 2,
        scratch_shapes=scratch + [pltpu.VMEM((tiles, 6 * rows, LANES), jnp.float32)],
        compiler_params=COMPACT,
        name="prepare",
    )(pair, near, far)


def chain(gap, old, z, coefs, powers, outs, rows, pads):
    slices = len(outs)
    n = lax.axis_index("cuts")
    own = slice(SUB + pads, SUB + pads + rows)
    extent = slice(*coarse_rows(STAGES * (slices - 1), rows, pads))
    for t in range(gap.shape[0]):
        start = jnp.where(n == 0, old[t, extent], 0.0)
        gap[t, extent] = (gap[t, extent] - old[t, extent]) + start
        mine = old[t, own]
        outs[-1][t] = jnp.where(n == 0, mine, 0.0) - mine
    reach = STAGES * (slices - 1)
    for j in range(1, slices):
        step(gap, z, coefs, [coarse_rows(reach - k, rows, pads) for k in range(1, STAGES + 1)], coarse_diffusion(), 1)
        reach -= STAGES
        for t in range(gap.shape[0]):
            powers[j, t] = gap[t, own]
    for out, table in zip(outs[:-1], partners(slices), strict=True):
        ahead = pick(n, [max(x - i, 1) for i, x in enumerate(table)])
        for t in range(gap.shape[0]):
            out[t] = powers[ahead, t]


def pair_chain_kernel(slices, rows, whole, message, passed, old, coefs, *refs):
    outs, (gap, z, powers, wide) = refs[:slices], refs[slices:]
    odd = band_of_pair() == 1
    pads = 2 * rows
    first = pl.multiple_of(rows * band_of_pair(), SUB)
    clear_edges((gap, z.at[0], z.at[1]))
    for t in range(gap.shape[0]):
        wide[t] = jnp.zeros(wide.shape[1:], jnp.float32)
        at = pads - SPILL
        wide[t, at : at + whole.shape[1]] = whole[t]
        for at, x in (
            (pads + SPILL - 2 * rows, jnp.where(odd, passed[t], message[t])),
            (pads - SPILL + 2 * rows, jnp.where(odd, message[t], passed[t])),
        ):
            wide[t, at : at + 2 * rows] = wide[t, at : at + 2 * rows] + x
        gap[t, SUB : SUB + rows + 2 * pads] = wide[t, pl.ds(first, rows + 2 * pads)]
    chain(gap, old, z, coefs, powers, outs, rows, pads)


def chain_shapes(tiles, size, slices, rows):
    f32 = jnp.float32
    return (
        (jax.ShapeDtypeStruct((tiles, rows, LANES), f32),) * slices,
        [
            pltpu.VMEM((tiles, size, LANES), f32),
            pltpu.VMEM((2, tiles, size, LANES), f32),
            pltpu.VMEM((slices, tiles, rows, LANES), f32),
        ],
    )


def pair_chain_call(slices, whole, message, passed, old, coefs):
    tiles = whole.shape[0]
    rows = message.shape[1] // 2
    shapes, scratch = chain_shapes(tiles, old.shape[1], slices, rows)
    return pl.pallas_call(
        functools.partial(pair_chain_kernel, slices, rows),
        out_shape=shapes,
        in_specs=[VMEM] * 5,
        out_specs=(VMEM,) * slices,
        scratch_shapes=scratch + [pltpu.VMEM((tiles, 6 * rows, LANES), jnp.float32)],
        compiler_params=COMPACT,
        name="coarse",
    )(whole, message, passed, old, coefs)


def wide_chain_kernel(slices, rows, pads, gap_in, old_in, psi_in, *refs):
    outs, (gap, z, powers, old, coefs, psi) = refs[:slices], refs[slices:]
    clear_edges((gap, old, psi, z.at[0], z.at[1]))
    for source, out in ((gap_in, gap), (old_in, old), (psi_in, psi)):
        for t in range(gap.shape[0]):
            out[t, SUB : SUB + rows + 2 * pads] = source[t]
    prepare(psi, old, z, coefs, rows, pads, slices)
    chain(gap, old, z, coefs, powers, outs, rows, pads)


def wide_chain(slices, spread, coarse):
    tiles, both, _ = coarse.shape
    rows = both // 2
    bands = lax.axis_size("space")
    total = bands * rows
    length = spread.shape[1]
    every = lax.all_gather(spread, "space")
    gap = jnp.zeros((tiles, total, LANES), jnp.float32)
    for b in range(bands):
        at = (b * rows - SPILL + jnp.arange(length)) % total
        gap = gap.at[:, at].add(every[b])
    every = lax.all_gather(coarse, "space")
    old, psi = (jnp.moveaxis(every[:, :, k * rows : (k + 1) * rows], 0, 1).reshape(tiles, total, LANES) for k in range(2))
    pads = -(-STAGES * slices // SUB) * SUB
    at = (lax.axis_index("space") * rows - pads + jnp.arange(rows + 2 * pads)) % total
    size = rows + 2 * pads + 2 * SUB
    shapes, scratch = chain_shapes(tiles, size, slices, rows)
    more = [pltpu.VMEM(x.shape, x.dtype) for x in prepare_shapes(tiles, size)[0]]
    return pl.pallas_call(
        functools.partial(wide_chain_kernel, slices, rows, pads),
        out_shape=shapes,
        in_specs=[VMEM] * 3,
        out_specs=(VMEM,) * slices,
        scratch_shapes=scratch + more + [pltpu.VMEM((tiles, size, LANES), jnp.float32)],
        compiler_params=COMPACT,
        name="coarse",
    )(*(jnp.take(x, at, axis=1) for x in (gap, old, psi)))


def settle_kernel(fine, from_twin, from_across, out, tall):
    tiles, rows, _ = fine.shape
    odd = band_of_pair() == 1
    for t in range(tiles):
        tall[t, 0:REACH] = fine[t, 0:REACH] + jnp.where(odd, from_twin[t], from_across[t])
        tall[t, REACH : rows - REACH] = fine[t, REACH : rows - REACH]
        tall[t, rows - REACH : rows] = fine[t, rows - REACH : rows] + jnp.where(odd, from_across[t], from_twin[t])
    for k in range(0, tiles, BLOCK):
        for i, x in enumerate(in_order([tall[k + i] for i in range(BLOCK)])):
            out[:, (k + i) * LANES : (k + i + 1) * LANES] = x


def settle_call(fine, from_twin, from_across):
    tiles, rows, _ = fine.shape
    return pl.pallas_call(
        settle_kernel,
        out_shape=jax.ShapeDtypeStruct((rows, tiles * LANES), jnp.float32),
        in_specs=[VMEM] * 3,
        out_specs=VMEM,
        scratch_shapes=[pltpu.VMEM((tiles, rows, LANES), jnp.float32)],
        compiler_params=COMPACT,
        name="settle",
    )(fine, from_twin, from_across)


def out_kernel(slices, fine, own, *refs):
    received, (out, tall) = refs[: slices - 1], refs[slices - 1 :]
    rows, cols = fine.shape
    count = rows // BLOCK
    n = lax.axis_index("cuts")
    lane = lane_index((count, LANES))
    per = LANES // BLOCK
    sources = [pick(n, [table.index(i) for i in range(slices)]) for table in partners(slices)]
    for k in range(cols // LANES // BLOCK):
        total = own[k]
        for source, x in zip(sources, received, strict=True):
            total = total + jnp.where(source < n, x[k], 0.0)
        for q in range(BLOCK):
            t = k * BLOCK + q
            up = jnp.take_along_axis(total, q * per + lane // BLOCK, axis=1)
            for i in range(BLOCK):
                tall[t, pl.ds(i, count, stride=BLOCK)] = up
            at = slice(t * LANES, (t + 1) * LANES)
            out[0, :, at] = fine[:, at] + tall[t]


def out_call(slices, fine, own, received):
    rows, cols = fine.shape
    return pl.pallas_call(
        functools.partial(out_kernel, slices),
        out_shape=jax.ShapeDtypeStruct((1, rows, cols), jnp.float32),
        in_specs=[VMEM] * (1 + slices),
        out_specs=VMEM,
        scratch_shapes=[pltpu.VMEM((cols // LANES, rows, LANES), jnp.float32)],
        compiler_params=COMPACT,
        name="total",
    )(fine, own, *received)


def iteration(states, stream):
    state = states[0]
    slices, bands = lax.axis_size("cuts"), lax.axis_size("space")
    rows = state.shape[0] // BLOCK
    twin = [(i, i ^ 1) for i in range(bands)]
    across = [(i, (i + 1 if i % 2 else i - 1) % bands) for i in range(bands)]

    def exchange(x, pairs):
        return lax.ppermute(x, "space", pairs)

    to_twin, to_across, state, stream = rows_call(state, stream)
    rows_across, rows_twin = exchange(to_across, across), exchange(to_twin, twin)
    coarse = restrict_call(state, stream)
    paired = STAGES * (slices - 1) <= 2 * rows - SPILL and STAGES * slices <= 2 * rows
    if paired:
        pair = pair_call(coarse, exchange(coarse, twin))
        pair_near = exchange(pair, across)
        pair_far = exchange(pair_near, twin)
    tall = interleave_call(state, stream)
    begun = inside_call(*tall, rows_twin)
    fine, edge_twin, edge_across, spread = fine_call(rows_across, *begun, state.shape[0])
    if paired:
        whole, message = spread_call(spread, exchange(spread, twin), rows)
        near = exchange(message, across)
        far = exchange(near, twin)
        old, coefs = pair_prepare_call(slices, pair, pair_near, pair_far)
        *sent, own = pair_chain_call(slices, whole, near, far, old, coefs)
    else:
        *sent, own = wide_chain(slices, spread, coarse)
    from_twin, from_across = exchange(edge_twin, twin), exchange(edge_across, across)
    received = []
    for x, table in zip(sent, partners(slices), strict=True):
        received.append(lax.ppermute(x, "cuts", list(enumerate(table))))
    return out_call(slices, settle_call(fine, from_twin, from_across), own, received)


def solution(mesh):
    return jax.shard_map(
        iteration,
        mesh=mesh,
        in_specs=(P("cuts", "space", None), P("space", None)),
        out_specs=P("cuts", "space", None),
        check_vma=False,
    )
```
